1024 devices in a mesh: ctx: 64 (over y, x), head: 16 (over z, core).
Axes of the slice: x: 8, y: 8, z: 8, core: 2. Of those that a mesh axis runs over, the one named last changes fastest.
Arguments:
- queries: bfloat16 [4096, 128, 192], P('ctx', 'head'), may hold values from -84 to 84
- latent_keys: bfloat16 [4096, 576], P('ctx'), may hold values from -12 to 12
- out_grad: bfloat16 [4096, 128, 128], P('ctx', 'head'), may hold values from -6 to 6
- up_weight: bfloat16 [512, 128, 256], P(None, 'head'), may hold values from -0.25 to 0.25
- segment_ids: int32 [4096], replicated, may hold values from 0 to 127, never falling along the last dimension, each value on 1 to 64 neighbouring positions
Outputs:
- query_grad: float32 [4096, 128, 192], P('ctx', 'head')
- key_grad: float32 [4096, 576], P('ctx', 'head')
- weight_grad: float32 [512, 128, 256], P('ctx', 'head')
The draws below stay inside these ranges and needn't reach their ends.
Inputs may be any that keep to these rules, and one draw needn't show every extreme that they name: `segment_ids`: segment numbers never fall along the slab; each trace has 1 to 64 tokens and one has exactly 64.
All inputs are finite; a program needn't handle non-finite values.
Results may differ from the reference program's by a relative error of at most 0.0053.
Values may be sent and summed in bfloat16 or wider, within the bound.
A program may use at most 32 MiB of HBM per device.

```python
import math
import jax
import jax.numpy as jnp
import numpy as np
from jax import lax

HEADS = 128
LAT = 512
ROPE = 64
PLAIN_WIDTH = 128
VDIM = 128
TOK_DEV = 64
REACH = 1
TOKENS = 4096
MOST = 64
SEGS = 128
N_CTX = 64


def shared_rope(key):
    base = jax.random.normal(jax.random.fold_in(key, 11), (TOKENS, ROPE), jnp.float32)
    return jnp.clip(base, -4.0, 4.0)


def draw_latent_keys(key, part):
    latent = jnp.clip(jax.random.normal(jax.random.fold_in(key, 3), (TOKENS, LAT), jnp.float32), -4.0, 4.0)
    order = jax.random.permutation(jax.random.fold_in(key, 5), N_CTX)
    row_block = jnp.arange(TOKENS) // TOK_DEV
    col_block = jnp.arange(LAT) // (LAT // N_CTX)
    boost = jnp.where(order[row_block][:, None] == col_block[None, :], 3.0, 1.0)
    latent = latent * boost
    rope = shared_rope(key)
    return jnp.concatenate([latent, rope], 1).astype(jnp.bfloat16)


def draw_queries(key, part):
    base = jax.random.normal(jax.random.fold_in(key, 7), (TOKENS, HEADS, PLAIN_WIDTH + ROPE), jnp.float32)
    base = jnp.clip(base, -4.0, 4.0)
    return base.astype(jnp.bfloat16)


def block_scale(own_key, dims, pieces, low, high):
    def one(axis_at, shards_of):
        heights = jax.random.uniform(jax.random.fold_in(jax.random.fold_in(own_key, 6), axis_at), (shards_of,), jnp.float32, low / len(pieces), high / len(pieces))
        return jnp.repeat(jnp.exp(heights), dims[axis_at] // shards_of).reshape((-1,) + (1,) * (len(dims) - axis_at - 1))

    loudness = one(*pieces[0])
    for cut in pieces[1:]:
        loudness = loudness * one(*cut)
    return loudness


def profile(amount, total, most, skew):
    weights = [(1 << 20) // math.isqrt(rank ** skew) + 1 for rank in range(2, amount + 1)]
    spare, given = total - most - (amount - 1), [1] * (amount - 1)
    while spare > 0:
        movable = [i for i in range(amount - 1) if given[i] < most]
        pool, left = sum([weights[i] for i in movable]), spare
        for i in movable:
            addition = min(most - given[i], max(1, left * weights[i] // pool), spare)
            given[i] = given[i] + addition
            spare = spare - addition
    return np.array([most] + given)


def ragged_sizes(own_key, count, total, reach, lean):
    if count == 2:
        one = jax.random.randint(own_key, (), max(1, total - reach), min(reach, total - 1) + 1)
        return jnp.stack([one, total - one])
    sizes = jnp.asarray(profile(count, total, reach, lean), jnp.int32)
    couples = (count - 1) // 2
    source_of, taker = sizes[1:1 + 2 * couples:2], sizes[2:2 + 2 * couples:2]
    slack = jnp.minimum(source_of - 1, reach - taker)
    shifted = jax.random.randint(jax.random.fold_in(own_key, 1), (couples,), 0, 1 << 20) % (slack + 1)
    sizes = sizes.at[1:1 + 2 * couples:2].set(source_of - shifted).at[2:2 + 2 * couples:2].set(taker + shifted)
    return sizes[jax.random.permutation(jax.random.fold_in(own_key, 2), count)]


def noise(rng, shape, spread, bound, split=(), dtype=jnp.bfloat16):
    drawn = spread * jax.random.normal(rng, shape, jnp.float32)
    if split:
        drawn = drawn * block_scale(rng, shape, split, -0.22, 0.18)
    return jnp.clip(drawn, -bound, bound).astype(dtype)


def setup_inputs(seed: int = 0) -> dict:
    streams_of = jax.random.split(jax.random.key(seed), 6)
    return {
        "queries": draw_queries(jax.random.fold_in(streams_of[5], 71), 0),
        "latent_keys": draw_latent_keys(jax.random.fold_in(streams_of[5], 71), 0),
        "out_grad": noise(streams_of[2], (TOKENS, HEADS, VDIM), 1.0, 6.0, ((0, 64), (1, 16))),
        "up_weight": noise(streams_of[3], (LAT, HEADS, PLAIN_WIDTH + VDIM), LAT ** -0.5, 0.25, ((1, 16),)),
        "segment_ids": jnp.searchsorted(jnp.cumsum(ragged_sizes(streams_of[4], SEGS, TOKENS, MOST, 2)), jnp.arange(TOKENS), side="right").astype(jnp.int32),
    }


def fold_back(window_terms, nblk):
    shaped = window_terms.reshape((nblk, REACH + 1, TOK_DEV) + window_terms.shape[2:])
    total = jnp.zeros((nblk + REACH, TOK_DEV) + window_terms.shape[2:], jnp.float32)
    for j in range(REACH + 1):
        total = total.at[j:j + nblk].add(shaped[:, j])
    return total[REACH:].reshape((nblk * TOK_DEV,) + window_terms.shape[2:])

def reference(queries, latent_keys, out_grad, up_weight, segment_ids):
    scale = 1.0 / math.sqrt(PLAIN_WIDTH + ROPE)
    nblk = TOKENS // TOK_DEV
    width = (REACH + 1) * TOK_DEV
    group = 8
    ngroups = HEADS // group
    starts = (jnp.arange(nblk) * TOK_DEV).astype(jnp.int32)
    pad_keys = jnp.concatenate([jnp.zeros((REACH * TOK_DEV, LAT + ROPE), jnp.bfloat16), latent_keys], 0)
    pad_seg = jnp.concatenate([jnp.full((REACH * TOK_DEV,), -1, jnp.int32), segment_ids.astype(jnp.int32)], 0)
    windows = jax.vmap(lambda s: lax.dynamic_slice_in_dim(pad_keys, s, width, 0))(starts)
    seg_win = jax.vmap(lambda s: lax.dynamic_slice_in_dim(pad_seg, s, width, 0))(starts)
    seg_query = segment_ids.astype(jnp.int32).reshape(nblk, TOK_DEV)
    pos_key = jnp.arange(width)[None, :]
    pos_query = (jnp.arange(TOK_DEV) + REACH * TOK_DEV)[:, None]
    mask = (seg_query[:, :, None] == seg_win[:, None, :]) & (pos_key <= pos_query)[None]
    rotary_key_part = windows[..., LAT:].astype(jnp.float32)
    window_latent = windows[..., :LAT].astype(jnp.float32)
    q_groups = jnp.moveaxis(queries.reshape(TOKENS, ngroups, group, PLAIN_WIDTH + ROPE), 1, 0)
    g_groups = jnp.moveaxis(out_grad.reshape(TOKENS, ngroups, group, VDIM), 1, 0)
    w_groups = jnp.moveaxis(up_weight.reshape(LAT, ngroups, group, PLAIN_WIDTH + VDIM), 1, 0)

    def one_group(operands):
        q_g, g_g, w_g = operands
        flat_w = w_g.reshape(LAT, group * (PLAIN_WIDTH + VDIM))
        kv_tok = jnp.dot(latent_keys[:, :LAT], flat_w, preferred_element_type=jnp.float32).astype(jnp.bfloat16)
        pad_kv = jnp.concatenate([jnp.zeros((REACH * TOK_DEV, kv_tok.shape[1]), jnp.bfloat16), kv_tok], 0)
        kv_win = jax.vmap(lambda s: lax.dynamic_slice_in_dim(pad_kv, s, width, 0))(starts)
        kv_win = kv_win.reshape(nblk, width, group, PLAIN_WIDTH + VDIM).astype(jnp.float32)
        plain_key_part = kv_win[..., :PLAIN_WIDTH]
        values = kv_win[..., PLAIN_WIDTH:]
        query_up_matrix = q_g.reshape(nblk, TOK_DEV, group, PLAIN_WIDTH + ROPE).astype(jnp.float32)
        g_b = g_g.reshape(nblk, TOK_DEV, group, VDIM).astype(jnp.float32)
        attention_logits = jnp.einsum('zlmy,zcmy->zmlc', query_up_matrix[..., :PLAIN_WIDTH], plain_key_part) + jnp.einsum('pein,pmn->piem', query_up_matrix[..., PLAIN_WIDTH:], rotary_key_part)
        attention_logits = attention_logits * scale
        attention_logits = jnp.where(mask[:, None], attention_logits, -1e+30)
        top = lax.optimization_barrier(jnp.max(attention_logits, -1, keepdims=True))
        expo = jnp.where(mask[:, None], jnp.exp(attention_logits - top), 0.0)
        probs = expo / lax.optimization_barrier(jnp.sum(expo, -1, keepdims=True))
        dprobs = jnp.einsum('zlmy,zcmy->zmlc', g_b, values)
        delta = lax.optimization_barrier(jnp.sum(probs * dprobs, -1, keepdims=True))
        logit_gradient = lax.optimization_barrier((probs * (dprobs - delta) * scale).astype(jnp.bfloat16)).astype(jnp.float32)
        probs16 = lax.optimization_barrier(probs.astype(jnp.bfloat16)).astype(jnp.float32)
        query_gradient_rows = jnp.concatenate([jnp.einsum('zarp,zpay->zray', logit_gradient, plain_key_part), jnp.einsum('rnvc,rcj->rvnj', logit_gradient, rotary_key_part)], -1)
        dk = jnp.einsum('bhqk,bqhd->bkhd', logit_gradient, query_up_matrix[..., :PLAIN_WIDTH])
        dv = jnp.einsum('bhqk,bqhd->bkhd', probs16, g_b)
        rotary_key_gradient = jnp.einsum('vtau,vatc->vuc', logit_gradient, query_up_matrix[..., PLAIN_WIDTH:])
        dkv = lax.optimization_barrier(jnp.concatenate([dk, dv], -1).astype(jnp.bfloat16)).astype(jnp.float32)
        dkv_tok = fold_back(dkv, nblk).reshape(TOKENS, group * (PLAIN_WIDTH + VDIM))
        drope = fold_back(rotary_key_gradient, nblk)
        dlat = jnp.dot(dkv_tok, flat_w.astype(jnp.float32).T, precision=lax.Precision.HIGHEST)
        block_terms = jnp.einsum('bkl,bke->ble', window_latent, dkv.reshape(nblk, width, group * (PLAIN_WIDTH + VDIM)), precision=lax.Precision.HIGHEST)
        block_terms = lax.optimization_barrier(block_terms.astype(jnp.bfloat16)).astype(jnp.float32)
        dweight = lax.optimization_barrier(jnp.sum(block_terms, 0)).reshape(LAT, group, PLAIN_WIDTH + VDIM)
        return (query_gradient_rows.reshape(TOKENS, group, PLAIN_WIDTH + ROPE), jnp.concatenate([dlat, drope], -1), dweight)
    dq_all, dkeys_all, dw_all = lax.map(one_group, (q_groups, g_groups, w_groups))
    query_grad = jnp.moveaxis(dq_all, 0, 1).reshape(TOKENS, HEADS, PLAIN_WIDTH + ROPE)
    key_grad = lax.optimization_barrier(jnp.sum(dkeys_all, 0))
    weight_grad = jnp.moveaxis(dw_all, 0, 1).reshape(LAT, HEADS, PLAIN_WIDTH + VDIM)
    return (query_grad, key_grad, weight_grad)
```

```python
import math

import jax
import jax.numpy as jnp
from jax import lax
from jax.experimental import pallas as pl
from jax.experimental.pallas import tpu as pltpu
from jax.sharding import PartitionSpec as P

LAT = 512
ROPE = 64
NOPE = 128
VDIM = 128
KVD = NOPE + VDIM
TOK = 64
WIN = 128
HD = 8
L = 8
NH = 16
KROWS = 48
MESH = pl.DeviceIdType.MESH
F32 = jnp.float32
BF16 = jnp.bfloat16

STEPS = ((4, 0), (3, 1), (3, 0), (2, 1), (2, 0), (1, 1), (1, 0))


def dot(a, b, ca, cb):
    return lax.dot_general(a, b, (((ca,), (cb,)), ((), ())), preferred_element_type=F32)


def kernel(
    q_hbm, lat_hbm, do_hbm, w_hbm, seg_hbm,
    dq_hbm, kg_hbm, wg_hbm,
    q_v, do_v, w_v, seg_v, latwin,
    wf, wflat, qf, dof, dqf, dq_v,
    kv_v, dkv_v, ds_v, qr_v, kt32, kt16,
    term, ring, fin, part, kr, kpart, kprev, kg_v, wgf, wg_v,
    in_sem, halo_sem, ring_send, ring_recv, p2_send, p2_recv, k_send, k_recv, kp_sem, out_sem,
):
    c = lax.axis_index("ctx")
    h = lax.axis_index("head")
    y = lax.div(c, L)
    x = lax.rem(c, L)
    nxt = lax.rem(c + 1, L * L)
    prv = lax.rem(c + L * L - 1, L * L)

    def ctx_of(yy, xx):
        return yy * L + xx

    lat_cp = pltpu.make_async_copy(lat_hbm, latwin.at[pl.ds(TOK, TOK)], in_sem.at[0])
    w_cp = pltpu.make_async_copy(w_hbm, w_v, in_sem.at[1])
    q_cp = pltpu.make_async_copy(q_hbm, q_v, in_sem.at[2])
    do_cp = pltpu.make_async_copy(do_hbm, do_v, in_sem.at[3])
    seg_cp = pltpu.make_async_copy(seg_hbm, seg_v, in_sem.at[4])
    for cp in (lat_cp, w_cp, q_cp, do_cp, seg_cp):
        cp.start()

    barrier = pltpu.get_barrier_semaphore()
    pl.semaphore_signal(barrier, inc=1, device_id=(nxt, h), device_id_type=MESH)
    pl.semaphore_signal(barrier, inc=1, device_id=(prv, h), device_id_type=MESH)
    for d in range(1, L):
        pl.semaphore_signal(
            barrier, inc=1, device_id=(ctx_of(y, lax.rem(x + d, L)), h), device_id_type=MESH
        )
        pl.semaphore_signal(
            barrier, inc=1, device_id=(ctx_of(lax.rem(y + d, L), x), h), device_id_type=MESH
        )
    for d in range(1, NH):
        pl.semaphore_signal(
            barrier, inc=1, device_id=(c, lax.rem(h + d, NH)), device_id_type=MESH
        )

    q_cp.wait()
    do_cp.wait()
    qf[1] = jnp.zeros((TOK * HD, 128), F32)
    qf[0] = q_v[:, :NOPE].astype(F32)
    qf[1, :, :ROPE] = q_v[:, NOPE:].astype(F32)
    dof[...] = do_v[...].astype(F32)
    qn, dob = [], []
    for hd in range(HD):
        qn.append(qf[0, pl.ds(hd, TOK, stride=HD), :].astype(BF16))
        qr_v[pl.ds(hd * TOK, TOK), :] = qf[1, pl.ds(hd, TOK, stride=HD), :].astype(BF16)
        dob.append(dof[pl.ds(hd, TOK, stride=HD), :].astype(BF16))

    lat_cp.wait()
    pl.semaphore_wait(barrier, 2 + 2 * (L - 1) + NH - 1)
    halo = pltpu.make_async_remote_copy(
        src_ref=latwin.at[pl.ds(TOK, TOK)],
        dst_ref=latwin.at[pl.ds(0, TOK)],
        send_sem=halo_sem.at[0],
        recv_sem=halo_sem.at[1],
        device_id=(nxt, h),
        device_id_type=MESH,
    )
    halo.start()

    w_cp.wait()
    rows = LAT * HD // 8

    def relayout(i, carry):
        base = pl.multiple_of(i * rows, rows)
        out = pl.multiple_of(i * (LAT // 8), LAT // 8)
        for half in range(2):
            wf[half] = w_v[pl.ds(base, rows), half * 128 : (half + 1) * 128].astype(F32)
        for hd in range(HD):
            for half in range(2):
                wflat[hd, pl.ds(out, LAT // 8), half * 128 : (half + 1) * 128] = wf[
                    half, pl.ds(hd, LAT // 8, stride=HD), :
                ].astype(BF16)
        return carry

    lax.fori_loop(0, 8, relayout, 0)

    seg_cp.wait()
    row = lax.div(c, 2)
    odd = lax.rem(c, 2)
    lane = lax.broadcasted_iota(jnp.int32, (1, WIN), 1)
    row_a = seg_v[pl.ds(row, 1), :]
    row_b = seg_v[pl.ds(jnp.maximum(row - 1, 0), 1), :]
    mixed = pltpu.roll(jnp.where(lane >= TOK, row_b, row_a), TOK, 1)
    seg_row = jnp.where(odd == 1, row_a, mixed)
    seg_row = jnp.where((lane < TOK) & (c == 0), -1, seg_row).astype(F32)
    seg_all = jnp.broadcast_to(seg_row, (WIN, WIN))
    seg_col = seg_all.T[TOK:, :]
    seg_all = seg_all[:TOK, :]
    pos_key = lax.broadcasted_iota(jnp.int32, (TOK, WIN), 1)
    pos_query = lax.broadcasted_iota(jnp.int32, (TOK, WIN), 0) + TOK
    visible = (seg_col == seg_all) & (pos_key <= pos_query)

    for hd in range(HD):
        kv_v[hd, TOK:, :] = dot(latwin[TOK:, :LAT], wflat[hd], 1, 0).astype(BF16)
    halo.wait_recv()
    for hd in range(HD):
        kv_v[hd, :TOK, :] = dot(latwin[:TOK, :LAT], wflat[hd], 1, 0).astype(BF16)

    k_rope = jnp.concatenate([latwin[:, LAT:], jnp.zeros((WIN, 128 - ROPE), BF16)], 1)
    scale = 1.0 / math.sqrt(NOPE + ROPE)
    scores, dprobs = [], []
    for hd in range(HD):
        key = kv_v[hd, :, :NOPE]
        val = kv_v[hd, :, NOPE:]
        q_rope = qr_v[pl.ds(hd * TOK, TOK), :]
        scores.append(dot(qn[hd], key, 1, 1) + dot(q_rope, k_rope, 1, 1))
        dprobs.append(dot(dob[hd], val, 1, 1))
    for hd in range(HD):
        s = jnp.where(visible, scores[hd] * scale, -1e30)
        top = jnp.max(s, -1, keepdims=True)
        expo = jnp.where(visible, jnp.exp(s - top), 0.0)
        probs = expo / jnp.sum(expo, -1, keepdims=True)
        delta = jnp.sum(probs * dprobs[hd], -1, keepdims=True)
        ds = (probs * (dprobs[hd] - delta) * scale).astype(BF16)
        p16 = probs.astype(BF16)
        ds_v[pl.ds(hd * TOK, TOK), :] = ds
        dkv_v[hd, :, :NOPE] = dot(ds, qn[hd], 0, 0).astype(BF16)
        dkv_v[hd, :, NOPE:] = dot(p16, dob[hd], 0, 0).astype(BF16)

    lat_t = latwin[:, :LAT].T

    def terms(part_id):
        for side in range(2):
            a = 4 * part_id + side
            lo = dot(lat_t, dkv_v[a], 1, 0).reshape(L * L, 8, KVD)
            hi = dot(lat_t, dkv_v[a + 2], 1, 0).reshape(L * L, 8, KVD)
            both = jnp.concatenate([lo, hi], 1).astype(BF16).reshape(L, L, 16, KVD)
            for i in range(L):
                block = both[:, i] if part_id == 0 else both[i]
                term[part_id, i, :, :, side * KVD : (side + 1) * KVD] = block

    def place(part_id, sign, dist):
        pos = x if part_id == 0 else y
        return lax.rem(pos + sign * dist + L, L)

    def neighbour(part_id, sign):
        if part_id == 0:
            return (ctx_of(y, lax.rem(x + sign + L, L)), h)
        return (ctx_of(lax.rem(y + sign + L, L), x), h)

    def message(g, m):
        part_id, back = g // 2, g % 2
        sign = -1 if back else 1
        dist, half = STEPS[m]
        half = half ^ back
        src = term.at[part_id, place(part_id, sign, dist), pl.ds(4 * half, 4)]
        dst = fin.at[g, pl.ds(4 * half, 4)] if dist == 1 else ring.at[g, m]
        return pltpu.make_async_remote_copy(
            src_ref=src,
            dst_ref=dst,
            send_sem=ring_send.at[g, m],
            recv_sem=ring_recv.at[g, m],
            device_id=neighbour(part_id, sign),
            device_id_type=MESH,
        )

    def add(g, m):
        part_id, back = g // 2, g % 2
        sign = -1 if back else 1
        dist, half = STEPS[m]
        half = half ^ back
        at = place(part_id, sign, dist)
        own = term[part_id, at, pl.ds(4 * half, 4)].astype(F32)
        term[part_id, at, pl.ds(4 * half, 4)] = (own + ring[g, m - 2].astype(F32)).astype(BF16)

    for part_id in range(2):
        terms(part_id)
        for g in (2 * part_id, 2 * part_id + 1):
            message(g, 0).start()
            message(g, 1).start()

    acc = dot(wflat[0], dkv_v[0], 1, 1)
    for hd in range(1, HD):
        acc = acc + dot(wflat[hd], dkv_v[hd], 1, 1)
    kt32[pl.ds(0, LAT), :] = acc
    kt32[pl.ds(LAT, ROPE), :] = dot(qr_v[...], ds_v[...], 0, 0)[:ROPE, :]
    kt16[...] = kt32[...].astype(BF16)

    def k_start(to):
        return pl.multiple_of(lax.div(36 * to, 16) * 16, 16)

    k_copies = []
    for d in range(1, NH):
        to = lax.rem(h + d, NH)
        cp = pltpu.make_async_remote_copy(
            src_ref=kt16.at[pl.ds(k_start(to), KROWS)],
            dst_ref=kr.at[d],
            send_sem=k_send.at[d],
            recv_sem=k_recv.at[d],
            device_id=(c, to),
            device_id_type=MESH,
        )
        cp.start()
        k_copies.append(cp)

    for m in range(2, 4):
        for g in range(4):
            message(g, m - 2).wait_recv()
            add(g, m)
            message(g, m).start()

    for hd in range(HD):
        ds = ds_v[pl.ds(hd * TOK, TOK), :]
        dqf[0, pl.ds(hd, TOK, stride=HD), :] = dot(ds, kv_v[hd, :, :NOPE], 1, 0)
        dqf[1, pl.ds(hd, TOK, stride=HD), :] = dot(ds, k_rope, 1, 0)
    dq_v[:, :NOPE] = dqf[0]
    dq_v[:, NOPE:] = dqf[1, :, :ROPE]
    dq_out = pltpu.make_async_copy(dq_v, dq_hbm, out_sem.at[0])
    dq_out.start()

    for m in range(4, 5):
        for g in range(4):
            message(g, m - 2).wait_recv()
            add(g, m)
            message(g, m).start()

    total = kt32[pl.ds(k_start(h), KROWS), :]
    for d in range(1, NH):
        k_copies[d - 1].wait_recv()
        total = total + kr[d].astype(F32)
    kpart[...] = total
    kp = pltpu.make_async_remote_copy(
        src_ref=kpart,
        dst_ref=kprev,
        send_sem=kp_sem.at[0],
        recv_sem=kp_sem.at[1],
        device_id=(prv, h),
        device_id_type=MESH,
    )
    kp.start()

    for m in range(5, 7):
        for g in range(4):
            message(g, m - 2).wait_recv()
            add(g, m)
            message(g, m).start()

    kp.wait_recv()
    both = kpart[...] + pltpu.roll(kprev[...], TOK, 1)
    flip = jnp.concatenate([both, jnp.zeros((128 - KROWS, 128), F32)], 0).T[TOK:, :]
    off = lax.rem(36 * h, 16)
    pick = flip
    for o in (4, 8, 12):
        pick = jnp.where(off == o, pltpu.roll(flip, 128 - o, 1), pick)
    kg_v[...] = pick[:, :36]
    kg_out = pltpu.make_async_copy(kg_v, kg_hbm, out_sem.at[1])
    kg_out.start()

    def p2(part_id, to, frm):
        dev = (ctx_of(to, x), h) if part_id == 0 else (ctx_of(y, to), h)
        return pltpu.make_async_remote_copy(
            src_ref=term.at[part_id, x if part_id == 0 else y, to],
            dst_ref=part.at[part_id, frm],
            send_sem=p2_send.at[part_id, to],
            recv_sem=p2_recv.at[part_id, frm],
            device_id=dev,
            device_id_type=MESH,
        )

    for part_id in range(2):
        mine = x if part_id == 0 else y
        pos = y if part_id == 0 else x
        for back in range(2):
            for m in (5, 6):
                message(2 * part_id + back, m).wait_recv()
        wgf[part_id] = (
            term[part_id, mine, pos].astype(F32)
            + fin[2 * part_id, pos].astype(F32)
            + fin[2 * part_id + 1, pos].astype(F32)
        )
        summed = (
            term[part_id, mine].astype(F32)
            + fin[2 * part_id].astype(F32)
            + fin[2 * part_id + 1].astype(F32)
        )
        term[part_id, mine] = summed.astype(BF16)
        for d in range(1, L):
            p2(part_id, lax.rem(pos + d, L), pos).start()

    for part_id in range(2):
        pos = y if part_id == 0 else x
        total = wgf[part_id]
        for d in range(1, L):
            frm = lax.rem(pos + d, L)
            p2(part_id, frm, frm).wait_recv()
            total = total + part[part_id, frm].astype(F32)
        for a in range(4):
            rows0 = (a // 2) * 8
            for half in range(2):
                cols = (a % 2) * KVD + half * 128
                wg_v[half, pl.ds(4 * part_id + a, 8, stride=HD), :] = total[
                    rows0 : rows0 + 8, cols : cols + 128
                ]
    wg_outs = []
    for half in range(2):
        cp = pltpu.make_async_copy(
            wg_v.at[half], wg_hbm.at[:, pl.ds(half * 128, 128)], out_sem.at[2 + half]
        )
        cp.start()
        wg_outs.append(cp)

    halo.wait_send()
    kp.wait_send()
    for cp in k_copies:
        cp.wait_send()
    for g in range(4):
        for m in range(len(STEPS)):
            message(g, m).wait_send()
    for part_id in range(2):
        pos = y if part_id == 0 else x
        for d in range(1, L):
            p2(part_id, lax.rem(pos + d, L), pos).wait_send()
    for cp in (dq_out, kg_out, *wg_outs):
        cp.wait()


def shards(queries, latent_keys, out_grad, up_weight, segment_ids):
    vm, dma = pltpu.VMEM, pltpu.SemaphoreType.DMA
    dq, kg, wg = pl.pallas_call(
        kernel,
        out_shape=(
            jax.ShapeDtypeStruct((TOK * HD, NOPE + ROPE), F32),
            jax.ShapeDtypeStruct((TOK, 36), F32),
            jax.ShapeDtypeStruct((64, KVD), F32),
        ),
        in_specs=[pl.BlockSpec(memory_space=pl.ANY)] * 5,
        out_specs=[pl.BlockSpec(memory_space=pl.ANY)] * 3,
        scratch_shapes=[
            vm((TOK * HD, NOPE + ROPE), BF16),
            vm((TOK * HD, VDIM), BF16),
            vm((LAT * HD, KVD), BF16),
            vm((32, 128), jnp.int32),
            vm((WIN, LAT + ROPE), BF16),
            vm((2, LAT, 128), F32),
            vm((HD, LAT, KVD), BF16),
            vm((2, TOK * HD, 128), F32),
            vm((TOK * HD, VDIM), F32),
            vm((2, TOK * HD, 128), F32),
            vm((TOK * HD, NOPE + ROPE), F32),
            vm((HD, WIN, KVD), BF16),
            vm((HD, WIN, KVD), BF16),
            vm((HD * TOK, WIN), BF16),
            vm((HD * TOK, 128), BF16),
            vm((LAT + ROPE, WIN), F32),
            vm((LAT + ROPE, WIN), BF16),
            vm((2, L, L, 16, 512), BF16),
            vm((4, 5, 4, 16, 512), BF16),
            vm((4, L, 16, 512), BF16),
            vm((2, L, 16, 512), BF16),
            vm((NH, KROWS, WIN), BF16),
            vm((KROWS, WIN), F32),
            vm((KROWS, WIN), F32),
            vm((TOK, 36), F32),
            vm((2, 16, 512), F32),
            vm((2, 64, 128), F32),
            dma((5,)),
            dma((2,)),
            dma((4, 7)),
            dma((4, 7)),
            dma((2, L)),
            dma((2, L)),
            dma((NH,)),
            dma((NH,)),
            dma((2,)),
            dma((4,)),
        ],
        compiler_params=pltpu.CompilerParams(collective_id=0, has_side_effects=True),
        name="mla_backward",
    )(
        queries.reshape(TOK * HD, NOPE + ROPE),
        latent_keys,
        out_grad.reshape(TOK * HD, VDIM),
        up_weight.reshape(LAT * HD, KVD),
        segment_ids.reshape(32, 128),
    )
    return (
        dq.reshape(TOK, HD, NOPE + ROPE),
        kg,
        wg.reshape(8, HD, KVD),
    )


def solution(mesh):
    return jax.shard_map(
        shards,
        mesh=mesh,
        in_specs=(
            P("ctx", "head", None),
            P("ctx", None),
            P("ctx", "head", None),
            P(None, "head", None),
            P(),
        ),
        out_specs=(P("ctx", "head", None), P("ctx", "head"), P("ctx", "head", None)),
        check_vma=False,
    )
```

```python
import math

import jax
import jax.numpy as jnp
from jax import lax
from jax.experimental import pallas as pl
from jax.experimental.pallas import tpu as pltpu
from jax.sharding import PartitionSpec as P

LAT = 512
ROPE = 64
NOPE = 128
VDIM = 128
KVD = NOPE + VDIM
TOK = 64
WIN = 128
HD = 8
L = 8
NH = 16
KROWS = 48
MESH = pl.DeviceIdType.MESH
F32 = jnp.float32
BF16 = jnp.bfloat16

STEPS = (
    (4, 0), (4, 1), (3, 2), (3, 3), (3, 0), (3, 1), (2, 2),
    (2, 3), (2, 0), (2, 1), (1, 2), (1, 3), (1, 0), (1, 1),
)
LAG = 4


def dot(a, b, ca, cb):
    return lax.dot_general(a, b, (((ca,), (cb,)), ((), ())), preferred_element_type=F32)


def kernel(
    q_hbm, lat_hbm, do_hbm, w_hbm, seg_hbm,
    dq_v, kg_v, wg_v,
    q_v, do_v, w_v, seg_v, latwin,
    wf, wflat, qf, dof, dqf,
    kv_v, dkv_v, ds_v, qr_v, kt32, kt16,
    term, ring, fin, part, kr, kpart, kprev, wgf, wgs,
    plane_sem, z_sem, in_sem, halo_sem, ring_send, ring_recv, p2_send, p2_recv, k_send, k_recv, kp_sem,
):
    c = lax.axis_index("ctx")
    h = lax.axis_index("head")
    y = lax.div(c, L)
    x = lax.rem(c, L)
    nxt = lax.rem(c + 1, L * L)
    prv = lax.rem(c + L * L - 1, L * L)

    def ctx_of(yy, xx):
        return yy * L + xx

    lat_cp = pltpu.make_async_copy(lat_hbm, latwin.at[pl.ds(TOK, TOK)], in_sem.at[0])
    w_cp = pltpu.make_async_copy(w_hbm, w_v, in_sem.at[1])
    q_cp = pltpu.make_async_copy(q_hbm, q_v, in_sem.at[2])
    do_cp = pltpu.make_async_copy(do_hbm, do_v, in_sem.at[3])
    seg_cp = pltpu.make_async_copy(seg_hbm, seg_v, in_sem.at[4])
    for cp in (lat_cp, w_cp, q_cp, do_cp, seg_cp):
        cp.start()

    core = lax.rem(h, 2)
    z = lax.div(h, 2)
    chip0, chip1 = (c, 2 * z), (c, 2 * z + 1)
    barrier = pltpu.get_barrier_semaphore()
    for to in (nxt, prv):
        pl.semaphore_signal(barrier, inc=1, device_id=(to, 2 * z), device_id_type=MESH)
    for d in range(1, L):
        for to in (ctx_of(y, lax.rem(x + d, L)), ctx_of(lax.rem(y + d, L), x)):
            pl.semaphore_signal(barrier, inc=1, device_id=(to, 2 * z), device_id_type=MESH)

    @pl.when(core == 1)
    def _():
        pl.semaphore_signal(barrier, inc=1, device_id=chip0, device_id_type=MESH)

    for d in range(1, NH // 2):
        pl.semaphore_signal(
            barrier,
            inc=1,
            device_id=(c, 2 * lax.rem(z + d, NH // 2) + 1),
            device_id_type=MESH,
        )

    q_cp.wait()
    do_cp.wait()
    qf[1] = jnp.zeros((TOK * HD, 128), F32)
    qf[0] = q_v[:, :NOPE].astype(F32)
    qf[1, :, :ROPE] = q_v[:, NOPE:].astype(F32)
    dof[...] = do_v[...].astype(F32)
    qn, dob = [], []
    for hd in range(HD):
        qn.append(qf[0, pl.ds(hd, TOK, stride=HD), :].astype(BF16))
        qr_v[pl.ds(hd * TOK, TOK), :] = qf[1, pl.ds(hd, TOK, stride=HD), :].astype(BF16)
        dob.append(dof[pl.ds(hd, TOK, stride=HD), :].astype(BF16))

    lat_cp.wait()

    @pl.when(core == 0)
    def _():
        pl.semaphore_wait(barrier, 2 * (2 + 2 * (L - 1)) + 1)
        pl.semaphore_signal(plane_sem, inc=1, device_id=chip1, device_id_type=MESH)

    @pl.when(core == 1)
    def _():
        pl.semaphore_wait(plane_sem, 1)

    halo = pltpu.make_async_remote_copy(
        src_ref=latwin.at[pl.ds(TOK, TOK)],
        dst_ref=latwin.at[pl.ds(0, TOK)],
        send_sem=halo_sem.at[0],
        recv_sem=halo_sem.at[1],
        device_id=(nxt, h),
        device_id_type=MESH,
    )
    halo.start()

    w_cp.wait()
    rows = LAT * HD // 8

    def relayout(i, carry):
        base = pl.multiple_of(i * rows, rows)
        out = pl.multiple_of(i * (LAT // 8), LAT // 8)
        for half in range(2):
            wf[half] = w_v[pl.ds(base, rows), half * 128 : (half + 1) * 128].astype(F32)
        for hd in range(HD):
            for half in range(2):
                wflat[hd, pl.ds(out, LAT // 8), half * 128 : (half + 1) * 128] = wf[
                    half, pl.ds(hd, LAT // 8, stride=HD), :
                ].astype(BF16)
        return carry

    lax.fori_loop(0, 8, relayout, 0)

    seg_cp.wait()
    row = lax.div(c, 2)
    odd = lax.rem(c, 2)
    lane = lax.broadcasted_iota(jnp.int32, (1, WIN), 1)
    row_a = seg_v[pl.ds(row, 1), :]
    row_b = seg_v[pl.ds(jnp.maximum(row - 1, 0), 1), :]
    mixed = pltpu.roll(jnp.where(lane >= TOK, row_b, row_a), TOK, 1)
    seg_row = jnp.where(odd == 1, row_a, mixed)
    seg_row = jnp.where((lane < TOK) & (c == 0), -1, seg_row).astype(F32)
    seg_all = jnp.broadcast_to(seg_row, (WIN, WIN))
    seg_col = seg_all.T[TOK:, :]
    seg_all = seg_all[:TOK, :]
    pos_key = lax.broadcasted_iota(jnp.int32, (TOK, WIN), 1)
    pos_query = lax.broadcasted_iota(jnp.int32, (TOK, WIN), 0) + TOK
    visible = (seg_col == seg_all) & (pos_key <= pos_query)

    for hd in range(HD):
        kv_v[hd, TOK:, :] = dot(latwin[TOK:, :LAT], wflat[hd], 1, 0).astype(BF16)
    halo.wait_recv()
    for hd in range(HD):
        kv_v[hd, :TOK, :] = dot(latwin[:TOK, :LAT], wflat[hd], 1, 0).astype(BF16)

    k_rope = jnp.concatenate([latwin[:, LAT:], jnp.zeros((WIN, 128 - ROPE), BF16)], 1)
    scale = 1.0 / math.sqrt(NOPE + ROPE)
    scores, dprobs = [], []
    for hd in range(HD):
        key = kv_v[hd, :, :NOPE]
        val = kv_v[hd, :, NOPE:]
        q_rope = qr_v[pl.ds(hd * TOK, TOK), :]
        scores.append(dot(qn[hd], key, 1, 1) + dot(q_rope, k_rope, 1, 1))
        dprobs.append(dot(dob[hd], val, 1, 1))
    for hd in range(HD):
        s = jnp.where(visible, scores[hd] * scale, -1e30)
        top = jnp.max(s, -1, keepdims=True)
        expo = jnp.where(visible, jnp.exp(s - top), 0.0)
        probs = expo / jnp.sum(expo, -1, keepdims=True)
        delta = jnp.sum(probs * dprobs[hd], -1, keepdims=True)
        ds = (probs * (dprobs[hd] - delta) * scale).astype(BF16)
        p16 = probs.astype(BF16)
        ds_v[pl.ds(hd * TOK, TOK), :] = ds
        dkv_v[hd, :, :NOPE] = dot(ds, qn[hd], 0, 0).astype(BF16)
        dkv_v[hd, :, NOPE:] = dot(p16, dob[hd], 0, 0).astype(BF16)

    lat_t = latwin[:, :LAT].T

    def terms(part_id):
        for side in range(2):
            a = 4 * part_id + side
            lo = dot(lat_t, dkv_v[a], 1, 0).reshape(L * L, 8, KVD)
            hi = dot(lat_t, dkv_v[a + 2], 1, 0).reshape(L * L, 8, KVD)
            both = jnp.concatenate([lo, hi], 1).astype(BF16).reshape(L, L, 16, KVD)
            for i in range(L):
                block = both[:, i] if part_id == 0 else both[i]
                term[part_id, i, :, :, side * KVD : (side + 1) * KVD] = block

    def place(part_id, sign, dist):
        pos = x if part_id == 0 else y
        return lax.rem(pos + sign * dist + L, L)

    def neighbour(part_id, sign):
        if part_id == 0:
            return (ctx_of(y, lax.rem(x + sign + L, L)), h)
        return (ctx_of(lax.rem(y + sign + L, L), x), h)

    def message(g, m):
        part_id, back = g // 2, g % 2
        sign = -1 if back else 1
        dist, quarter = STEPS[m]
        quarter = quarter ^ (2 * back)
        src = term.at[part_id, place(part_id, sign, dist), pl.ds(2 * quarter, 2)]
        dst = fin.at[g, pl.ds(2 * quarter, 2)] if dist == 1 else ring.at[g, m]
        return pltpu.make_async_remote_copy(
            src_ref=src,
            dst_ref=dst,
            send_sem=ring_send.at[g, m],
            recv_sem=ring_recv.at[g, m],
            device_id=neighbour(part_id, sign),
            device_id_type=MESH,
        )

    def add(g, m):
        part_id, back = g // 2, g % 2
        sign = -1 if back else 1
        dist, quarter = STEPS[m]
        quarter = quarter ^ (2 * back)
        at = place(part_id, sign, dist)
        own = term[part_id, at, pl.ds(2 * quarter, 2)].astype(F32)
        term[part_id, at, pl.ds(2 * quarter, 2)] = (own + ring[g, m - LAG].astype(F32)).astype(
            BF16
        )

    def advance(lo, hi):
        for m in range(lo, hi):
            for g in range(4):
                message(g, m - LAG).wait_recv()
                add(g, m)
                message(g, m).start()

    for part_id in range(2):
        terms(part_id)
        for g in (2 * part_id, 2 * part_id + 1):
            for m in range(LAG):
                message(g, m).start()

    acc = dot(wflat[0], dkv_v[0], 1, 1)
    for hd in range(1, HD):
        acc = acc + dot(wflat[hd], dkv_v[hd], 1, 1)
    kt32[pl.ds(0, LAT), :] = acc
    kt32[pl.ds(LAT, ROPE), :] = dot(qr_v[...], ds_v[...], 0, 0)[:ROPE, :]
    kt16[...] = kt32[...].astype(BF16)

    def k_start(to):
        return pl.multiple_of(lax.div(36 * to, 16) * 16, 16)

    def k_copy(d):
        to = lax.rem(h + d, NH)
        return pltpu.make_async_remote_copy(
            src_ref=kt16.at[pl.ds(k_start(to), KROWS)],
            dst_ref=kr.at[d],
            send_sem=k_send.at[d],
            recv_sem=k_recv.at[d],
            device_id=(c, to),
            device_id_type=MESH,
        )

    def k_exchange():
        @pl.when(core == 1)
        def _():
            pl.semaphore_wait(barrier, NH - 2)
            pl.semaphore_signal(z_sem, inc=1, device_id=chip0, device_id_type=MESH)

        @pl.when(core == 0)
        def _():
            pl.semaphore_wait(z_sem, 1)

        for d in range(1, NH):
            k_copy(d).start()

    pl.when(z >= 4)(k_exchange)

    for hd in range(HD):
        ds = ds_v[pl.ds(hd * TOK, TOK), :]
        dqf[0, pl.ds(hd, TOK, stride=HD), :] = dot(ds, kv_v[hd, :, :NOPE], 1, 0)
        dqf[1, pl.ds(hd, TOK, stride=HD), :] = dot(ds, k_rope, 1, 0)
    dq_v[:, :NOPE] = dqf[0]
    dq_v[:, NOPE:] = dqf[1, :, :ROPE]

    advance(LAG, 10)
    pl.when(z < 4)(k_exchange)
    advance(10, len(STEPS))

    def p2(part_id, to, frm):
        dev = (ctx_of(to, x), h) if part_id == 0 else (ctx_of(y, to), h)
        return pltpu.make_async_remote_copy(
            src_ref=term.at[part_id, x if part_id == 0 else y, to],
            dst_ref=part.at[part_id, frm],
            send_sem=p2_send.at[part_id, to],
            recv_sem=p2_recv.at[part_id, frm],
            device_id=dev,
            device_id_type=MESH,
        )

    def finish(part_id, quarter):
        mine = x if part_id == 0 else y
        pos = y if part_id == 0 else x
        at = pl.ds(2 * quarter, 2)
        summed = (
            term[part_id, mine, at].astype(F32)
            + fin[2 * part_id, at].astype(F32)
            + fin[2 * part_id + 1, at].astype(F32)
        )
        term[part_id, mine, at] = summed.astype(BF16)
        for j in range(2):
            to = 2 * quarter + j

            @pl.when(pos == to)
            def _():
                wgf[part_id] = summed[j]

            @pl.when(pos != to)
            def _():
                p2(part_id, to, pos).start()

    for last in range(2):
        for g in range(4):
            message(g, 10 + last).wait_recv()
            message(g, 12 + last).wait_recv()
        for part_id in range(2):
            finish(part_id, last)
            finish(part_id, 2 + last)

    total = kt32[pl.ds(k_start(h), KROWS), :]
    for d in range(1, NH):
        k_copy(d).wait_recv()
        total = total + kr[d].astype(F32)
    kpart[...] = total
    kp = pltpu.make_async_remote_copy(
        src_ref=kpart,
        dst_ref=kprev,
        send_sem=kp_sem.at[0],
        recv_sem=kp_sem.at[1],
        device_id=(prv, h),
        device_id_type=MESH,
    )
    kp.start()

    for part_id in range(2):
        pos = y if part_id == 0 else x
        total = wgf[part_id]
        for d in range(1, L):
            frm = lax.rem(pos + d, L)
            p2(part_id, frm, frm).wait_recv()
            total = total + part[part_id, frm].astype(F32)
        for a in range(4):
            rows0 = (a // 2) * 8
            for half in range(2):
                cols = (a % 2) * KVD + half * 128
                wgs[half, pl.ds(4 * part_id + a, 8, stride=HD), :] = total[
                    rows0 : rows0 + 8, cols : cols + 128
                ]
    wg_v[:, :128] = wgs[0]
    wg_v[:, 128:] = wgs[1]

    kp.wait_recv()
    both = pltpu.roll(kpart[...], TOK, 1) + kprev[...]
    off = lax.rem(36 * h, 16)
    pick = both
    for o in (4, 8, 12):
        pick = jnp.where(off == o, pltpu.roll(both, KROWS - o, 0), pick)
    kg_v[...] = pick[:36, :TOK]

    halo.wait_send()
    kp.wait_send()
    for d in range(1, NH):
        k_copy(d).wait_send()
    for g in range(4):
        for m in range(len(STEPS)):
            message(g, m).wait_send()
    for part_id in range(2):
        pos = y if part_id == 0 else x
        for d in range(1, L):
            p2(part_id, lax.rem(pos + d, L), pos).wait_send()


def hand_out(dq, kg, wg, dq_to, kg_to, wg_to, sem):
    copies = [
        pltpu.make_async_copy(src, dst, sem.at[i])
        for i, (src, dst) in enumerate(((dq, dq_to), (kg, kg_to), (wg, wg_to)))
    ]
    for cp in copies:
        cp.start()
    for cp in copies:
        cp.wait()


def shards(queries, latent_keys, out_grad, up_weight, segment_ids):
    vm, dma = pltpu.VMEM, pltpu.SemaphoreType.DMA
    dq, kg, wg = pl.pallas_call(
        kernel,
        out_shape=(
            jax.ShapeDtypeStruct((TOK * HD, NOPE + ROPE), F32),
            jax.ShapeDtypeStruct((36, TOK), F32),
            jax.ShapeDtypeStruct((64, KVD), F32),
        ),
        in_specs=[pl.BlockSpec(memory_space=pltpu.HBM)] * 5,
        out_specs=[pl.BlockSpec(memory_space=pltpu.VMEM)] * 3,
        scratch_shapes=[
            vm((TOK * HD, NOPE + ROPE), BF16),
            vm((TOK * HD, VDIM), BF16),
            vm((LAT * HD, KVD), BF16),
            vm((32, 128), jnp.int32),
            vm((WIN, LAT + ROPE), BF16),
            vm((2, LAT, 128), F32),
            vm((HD, LAT, KVD), BF16),
            vm((2, TOK * HD, 128), F32),
            vm((TOK * HD, VDIM), F32),
            vm((2, TOK * HD, 128), F32),
            vm((HD, WIN, KVD), BF16),
            vm((HD, WIN, KVD), BF16),
            vm((HD * TOK, WIN), BF16),
            vm((HD * TOK, 128), BF16),
            vm((LAT + ROPE, WIN), F32),
            vm((LAT + ROPE, WIN), BF16),
            vm((2, L, L, 16, 512), BF16),
            vm((4, 10, 2, 16, 512), BF16),
            vm((4, L, 16, 512), BF16),
            vm((2, L, 16, 512), BF16),
            vm((NH, KROWS, WIN), BF16),
            vm((KROWS, WIN), F32),
            vm((KROWS, WIN), F32),
            vm((2, 16, 512), F32),
            vm((2, 64, 128), F32),
            pltpu.SemaphoreType.REGULAR,
            pltpu.SemaphoreType.REGULAR,
            dma((5,)),
            dma((2,)),
            dma((4, len(STEPS))),
            dma((4, len(STEPS))),
            dma((2, L)),
            dma((2, L)),
            dma((NH,)),
            dma((NH,)),
            dma((2,)),
        ],
        compiler_params=pltpu.CompilerParams(
            collective_id=0, has_side_effects=True, vmem_limit_bytes=32 * 1024 * 1024
        ),
        name="mla_backward",
    )(
        *(
            pltpu.with_memory_space_constraint(a, pltpu.HBM)
            for a in (
                queries.reshape(TOK * HD, NOPE + ROPE),
                latent_keys,
                out_grad.reshape(TOK * HD, VDIM),
                up_weight.reshape(LAT * HD, KVD),
                segment_ids.reshape(32, 128),
            )
        )
    )
    dq, kg, wg = pl.pallas_call(
        hand_out,
        out_shape=tuple(jax.ShapeDtypeStruct(a.shape, a.dtype) for a in (dq, kg, wg)),
        in_specs=[pl.BlockSpec(memory_space=pl.ANY)] * 3,
        out_specs=[pl.BlockSpec(memory_space=pl.ANY)] * 3,
        scratch_shapes=[dma((3,))],
        compiler_params=pltpu.CompilerParams(vmem_limit_bytes=8 * 1024 * 1024),
        name="hand_out",
    )(dq, kg, wg)
    return (
        dq.reshape(TOK, HD, NOPE + ROPE),
        kg.T,
        wg.reshape(8, HD, KVD),
    )


def solution(mesh):
    return jax.shard_map(
        shards,
        mesh=mesh,
        in_specs=(
            P("ctx", "head", None),
            P("ctx", None),
            P("ctx", "head", None),
            P(None, "head", None),
            P(),
        ),
        out_specs=(P("ctx", "head", None), P("ctx", "head"), P("ctx", "head", None)),
        check_vma=False,
    )
```

```python
import math

import jax
import jax.numpy as jnp
from jax import lax
from jax.experimental import pallas as pl
from jax.experimental.pallas import tpu as pltpu
from jax.sharding import PartitionSpec as P

LAT = 512
ROPE = 64
NOPE = 128
VDIM = 128
KVD = NOPE + VDIM
TOK = 64
WIN = 128
HD = 8
L = 8
NH = 16
KROWS = 48
MESH = pl.DeviceIdType.MESH
F32 = jnp.float32
BF16 = jnp.bfloat16

STEPS = (
    (4, 0), (4, 1), (3, 2), (3, 3), (3, 0), (3, 1), (2, 2),
    (2, 3), (2, 0), (2, 1), (1, 2), (1, 3), (1, 0), (1, 1),
)
LAG = 4


def dot(a, b, ca, cb):
    return lax.dot_general(a, b, (((ca,), (cb,)), ((), ())), preferred_element_type=F32)


def kernel(
    q_hbm, lat_hbm, do_hbm, w_hbm, seg_hbm,
    dq_v, kg_v, wg_v,
    q_v, do_v, w_v, seg_v, latwin,
    wf, wflat, qf, dof, dqf,
    kv_v, dkv_v, ds_v, qr_v, kt32, kt16,
    term, ring, fin, part, kr, kpart, kprev, wgf, wgs,
    plane_sem, z_sem, in_sem, halo_sem, ring_send, ring_recv, p2_send, p2_recv, k_send, k_recv, kp_sem,
):
    c = lax.axis_index("ctx")
    h = lax.axis_index("head")
    y = lax.div(c, L)
    x = lax.rem(c, L)
    nxt = lax.rem(c + 1, L * L)
    prv = lax.rem(c + L * L - 1, L * L)

    def ctx_of(yy, xx):
        return yy * L + xx

    lat_cp = pltpu.make_async_copy(lat_hbm, latwin.at[pl.ds(TOK, TOK)], in_sem.at[0])
    w_cp = pltpu.make_async_copy(w_hbm, w_v, in_sem.at[1])
    q_cp = pltpu.make_async_copy(q_hbm, q_v, in_sem.at[2])
    do_cp = pltpu.make_async_copy(do_hbm, do_v, in_sem.at[3])
    seg_cp = pltpu.make_async_copy(seg_hbm, seg_v, in_sem.at[4])
    for cp in (lat_cp, q_cp, do_cp, seg_cp, w_cp):
        cp.start()

    core = lax.rem(h, 2)
    z = lax.div(h, 2)
    chip0, chip1 = (c, 2 * z), (c, 2 * z + 1)
    barrier = pltpu.get_barrier_semaphore()
    near = [nxt, prv]
    for d in (1, L - 1):
        near += [ctx_of(y, lax.rem(x + d, L)), ctx_of(lax.rem(y + d, L), x)]
    for to in near:
        pl.semaphore_signal(barrier, inc=1, device_id=(to, 2 * z), device_id_type=MESH)

    @pl.when(core == 1)
    def _():
        pl.semaphore_signal(barrier, inc=1, device_id=chip0, device_id_type=MESH)

    for d in range(1, NH // 2):
        pl.semaphore_signal(
            barrier,
            inc=1,
            device_id=(c, 2 * lax.rem(z + d, NH // 2) + 1),
            device_id_type=MESH,
        )

    lat_cp.wait()

    @pl.when(core == 0)
    def _():
        pl.semaphore_wait(barrier, 2 * len(near) + 1)
        pl.semaphore_signal(plane_sem, inc=1, device_id=chip1, device_id_type=MESH)

    @pl.when(core == 1)
    def _():
        pl.semaphore_wait(plane_sem, 1)

    halo = pltpu.make_async_remote_copy(
        src_ref=latwin.at[pl.ds(TOK, TOK)],
        dst_ref=latwin.at[pl.ds(0, TOK)],
        send_sem=halo_sem.at[0],
        recv_sem=halo_sem.at[1],
        device_id=(nxt, h),
        device_id_type=MESH,
    )
    first, final = c == 0, c == L * L - 1

    @pl.when(jnp.logical_not(final))
    def _():
        halo.start()

    @pl.when(first)
    def _():
        latwin[:TOK, :] = jnp.zeros((TOK, LAT + ROPE), BF16)

    q_cp.wait()
    do_cp.wait()
    qf[1] = jnp.zeros((TOK * HD, 128), F32)
    qf[0] = q_v[:, :NOPE].astype(F32)
    qf[1, :, :ROPE] = q_v[:, NOPE:].astype(F32)
    dof[...] = do_v[...].astype(F32)
    qn, dob = [], []
    for hd in range(HD):
        qn.append(qf[0, pl.ds(hd, TOK, stride=HD), :].astype(BF16))
        qr_v[pl.ds(hd * TOK, TOK), :] = qf[1, pl.ds(hd, TOK, stride=HD), :].astype(BF16)
        dob.append(dof[pl.ds(hd, TOK, stride=HD), :].astype(BF16))

    w_cp.wait()
    rows = LAT * HD // 8

    def relayout(i, carry):
        base = pl.multiple_of(i * rows, rows)
        out = pl.multiple_of(i * (LAT // 8), LAT // 8)
        for half in range(2):
            wf[half] = w_v[pl.ds(base, rows), half * 128 : (half + 1) * 128].astype(F32)
        for hd in range(HD):
            for half in range(2):
                wflat[hd, pl.ds(out, LAT // 8), half * 128 : (half + 1) * 128] = wf[
                    half, pl.ds(hd, LAT // 8, stride=HD), :
                ].astype(BF16)
        return carry

    lax.fori_loop(0, 8, relayout, 0)

    seg_cp.wait()
    row = lax.div(c, 2)
    odd = lax.rem(c, 2)
    lane = lax.broadcasted_iota(jnp.int32, (1, WIN), 1)
    row_a = seg_v[pl.ds(row, 1), :]
    row_b = seg_v[pl.ds(jnp.maximum(row - 1, 0), 1), :]
    mixed = pltpu.roll(jnp.where(lane >= TOK, row_b, row_a), TOK, 1)
    seg_row = jnp.where(odd == 1, row_a, mixed)
    seg_row = jnp.where((lane < TOK) & (c == 0), -1, seg_row).astype(F32)
    seg_all = jnp.broadcast_to(seg_row, (WIN, WIN))
    seg_col = seg_all.T[TOK:, :]
    seg_all = seg_all[:TOK, :]
    pos_key = lax.broadcasted_iota(jnp.int32, (TOK, WIN), 1)
    pos_query = lax.broadcasted_iota(jnp.int32, (TOK, WIN), 0) + TOK
    visible = (seg_col == seg_all) & (pos_key <= pos_query)

    for hd in range(HD):
        kv_v[hd, TOK:, :] = dot(latwin[TOK:, :LAT], wflat[hd], 1, 0).astype(BF16)

    @pl.when(jnp.logical_not(first))
    def _():
        halo.wait_recv()

    for hd in range(HD):
        kv_v[hd, :TOK, :] = dot(latwin[:TOK, :LAT], wflat[hd], 1, 0).astype(BF16)

    k_rope = jnp.concatenate([latwin[:, LAT:], jnp.zeros((WIN, 128 - ROPE), BF16)], 1)
    scale = 1.0 / math.sqrt(NOPE + ROPE)
    scores, dprobs = [], []
    for hd in range(HD):
        key = kv_v[hd, :, :NOPE]
        val = kv_v[hd, :, NOPE:]
        q_rope = qr_v[pl.ds(hd * TOK, TOK), :]
        scores.append(dot(qn[hd], key, 1, 1) + dot(q_rope, k_rope, 1, 1))
        dprobs.append(dot(dob[hd], val, 1, 1))
    for hd in range(HD):
        s = jnp.where(visible, scores[hd] * scale, -1e30)
        top = jnp.max(s, -1, keepdims=True)
        expo = jnp.where(visible, jnp.exp(s - top), 0.0)
        probs = expo / jnp.sum(expo, -1, keepdims=True)
        delta = jnp.sum(probs * dprobs[hd], -1, keepdims=True)
        ds = (probs * (dprobs[hd] - delta) * scale).astype(BF16)
        p16 = probs.astype(BF16)
        ds_v[pl.ds(hd * TOK, TOK), :] = ds
        dkv_v[hd, :, :NOPE] = dot(ds, qn[hd], 0, 0).astype(BF16)
        dkv_v[hd, :, NOPE:] = dot(p16, dob[hd], 0, 0).astype(BF16)

    lat_t = latwin[:, :LAT].T

    def terms(part_id):
        for side in range(2):
            a = 4 * part_id + side
            lo = dot(lat_t, dkv_v[a], 1, 0).reshape(L * L, 8, KVD)
            hi = dot(lat_t, dkv_v[a + 2], 1, 0).reshape(L * L, 8, KVD)
            both = jnp.concatenate([lo, hi], 1).astype(BF16).reshape(L, L, 16, KVD)
            for i in range(L):
                block = both[:, i] if part_id == 0 else both[i]
                term[part_id, i, :, :, side * KVD : (side + 1) * KVD] = block

    def place(part_id, sign, dist):
        pos = x if part_id == 0 else y
        return lax.rem(pos + sign * dist + L, L)

    def neighbour(part_id, sign):
        if part_id == 0:
            return (ctx_of(y, lax.rem(x + sign + L, L)), h)
        return (ctx_of(lax.rem(y + sign + L, L), x), h)

    def message(g, m):
        part_id, back = g // 2, g % 2
        sign = -1 if back else 1
        dist, quarter = STEPS[m]
        quarter = quarter ^ (2 * back)
        src = term.at[part_id, place(part_id, sign, dist), pl.ds(2 * quarter, 2)]
        dst = fin.at[g, pl.ds(2 * quarter, 2)] if dist == 1 else ring.at[g, m]
        return pltpu.make_async_remote_copy(
            src_ref=src,
            dst_ref=dst,
            send_sem=ring_send.at[g, m],
            recv_sem=ring_recv.at[g, m],
            device_id=neighbour(part_id, sign),
            device_id_type=MESH,
        )

    def add(g, m):
        part_id, back = g // 2, g % 2
        sign = -1 if back else 1
        dist, quarter = STEPS[m]
        quarter = quarter ^ (2 * back)
        at = place(part_id, sign, dist)
        own = term[part_id, at, pl.ds(2 * quarter, 2)].astype(F32)
        term[part_id, at, pl.ds(2 * quarter, 2)] = (own + ring[g, m - LAG].astype(F32)).astype(
            BF16
        )

    def advance(lo, hi):
        for m in range(lo, hi):
            for g in range(4):
                message(g, m - LAG).wait_recv()
                add(g, m)
                message(g, m).start()

    for part_id in range(2):
        terms(part_id)
        for g in (2 * part_id, 2 * part_id + 1):
            for m in range(LAG):
                message(g, m).start()

    acc = dot(wflat[0], dkv_v[0], 1, 1)
    for hd in range(1, HD):
        acc = acc + dot(wflat[hd], dkv_v[hd], 1, 1)
    kt32[pl.ds(0, LAT), :] = acc
    kt32[pl.ds(LAT, ROPE), :] = dot(qr_v[...], ds_v[...], 0, 0)[:ROPE, :]
    kt16[...] = kt32[...].astype(BF16)

    def k_start(to):
        return pl.multiple_of(lax.div(36 * to, 16) * 16, 16)

    def k_copy(d):
        to = lax.rem(h + d, NH)
        return pltpu.make_async_remote_copy(
            src_ref=kt16.at[pl.ds(k_start(to), KROWS)],
            dst_ref=kr.at[d],
            send_sem=k_send.at[d],
            recv_sem=k_recv.at[d],
            device_id=(c, to),
            device_id_type=MESH,
        )

    def k_exchange():
        @pl.when(core == 1)
        def _():
            pl.semaphore_wait(barrier, NH - 2)
            pl.semaphore_signal(z_sem, inc=1, device_id=chip0, device_id_type=MESH)

        @pl.when(core == 0)
        def _():
            pl.semaphore_wait(z_sem, 1)

        for d in range(1, NH):
            k_copy(d).start()

    pl.when(z >= 4)(k_exchange)

    for hd in range(HD):
        ds = ds_v[pl.ds(hd * TOK, TOK), :]
        dqf[0, pl.ds(hd, TOK, stride=HD), :] = dot(ds, kv_v[hd, :, :NOPE], 1, 0)
        dqf[1, pl.ds(hd, TOK, stride=HD), :] = dot(ds, k_rope, 1, 0)
    dq_v[:, :NOPE] = dqf[0]
    dq_v[:, NOPE:] = dqf[1, :, :ROPE]

    advance(LAG, 10)
    pl.when(z < 4)(k_exchange)
    advance(10, len(STEPS))

    def p2(part_id, to, frm):
        dev = (ctx_of(to, x), h) if part_id == 0 else (ctx_of(y, to), h)
        return pltpu.make_async_remote_copy(
            src_ref=term.at[part_id, x if part_id == 0 else y, to],
            dst_ref=part.at[part_id, frm],
            send_sem=p2_send.at[part_id, to],
            recv_sem=p2_recv.at[part_id, frm],
            device_id=dev,
            device_id_type=MESH,
        )

    def finish(part_id, quarter):
        mine = x if part_id == 0 else y
        pos = y if part_id == 0 else x
        at = pl.ds(2 * quarter, 2)
        summed = (
            term[part_id, mine, at].astype(F32)
            + fin[2 * part_id, at].astype(F32)
            + fin[2 * part_id + 1, at].astype(F32)
        )
        term[part_id, mine, at] = summed.astype(BF16)
        for j in range(2):
            to = 2 * quarter + j

            @pl.when(pos == to)
            def _():
                wgf[part_id] = summed[j]

            @pl.when(pos != to)
            def _():
                p2(part_id, to, pos).start()

    for last in range(2):
        for g in range(4):
            message(g, 10 + last).wait_recv()
            message(g, 12 + last).wait_recv()
        for part_id in range(2):
            finish(part_id, last)
            finish(part_id, 2 + last)

    total = kt32[pl.ds(k_start(h), KROWS), :]
    for d in range(1, NH):
        k_copy(d).wait_recv()
        total = total + kr[d].astype(F32)
    kpart[...] = total
    kp = pltpu.make_async_remote_copy(
        src_ref=kpart,
        dst_ref=kprev,
        send_sem=kp_sem.at[0],
        recv_sem=kp_sem.at[1],
        device_id=(prv, h),
        device_id_type=MESH,
    )

    @pl.when(jnp.logical_not(first))
    def _():
        kp.start()

    for part_id in range(2):
        pos = y if part_id == 0 else x
        total = wgf[part_id]
        for d in range(1, L):
            frm = lax.rem(pos + d, L)
            p2(part_id, frm, frm).wait_recv()
            total = total + part[part_id, frm].astype(F32)
        for a in range(4):
            rows0 = (a // 2) * 8
            for half in range(2):
                cols = (a % 2) * KVD + half * 128
                wgs[half, pl.ds(4 * part_id + a, 8, stride=HD), :] = total[
                    rows0 : rows0 + 8, cols : cols + 128
                ]
    wg_v[:, :128] = wgs[0]
    wg_v[:, 128:] = wgs[1]

    @pl.when(jnp.logical_not(final))
    def _():
        kp.wait_recv()

    @pl.when(final)
    def _():
        kprev[...] = jnp.zeros((KROWS, WIN), F32)

    both = pltpu.roll(kpart[...], TOK, 1) + kprev[...]
    off = lax.rem(36 * h, 16)
    pick = both
    for o in (4, 8, 12):
        pick = jnp.where(off == o, pltpu.roll(both, KROWS - o, 0), pick)
    kg_v[...] = pick[:36, :TOK]

    @pl.when(jnp.logical_not(final))
    def _():
        halo.wait_send()

    @pl.when(jnp.logical_not(first))
    def _():
        kp.wait_send()

    for d in range(1, NH):
        k_copy(d).wait_send()
    for g in range(4):
        for m in range(len(STEPS)):
            message(g, m).wait_send()
    for part_id in range(2):
        pos = y if part_id == 0 else x
        for d in range(1, L):
            p2(part_id, lax.rem(pos + d, L), pos).wait_send()


def hand_out(dq, kg, wg, dq_to, kg_to, wg_to, sem):
    copies = [
        pltpu.make_async_copy(src, dst, sem.at[i])
        for i, (src, dst) in enumerate(((dq, dq_to), (kg, kg_to), (wg, wg_to)))
    ]
    for cp in copies:
        cp.start()
    for cp in copies:
        cp.wait()


def shards(queries, latent_keys, out_grad, up_weight, segment_ids):
    vm, dma = pltpu.VMEM, pltpu.SemaphoreType.DMA
    dq, kg, wg = pl.pallas_call(
        kernel,
        out_shape=(
            jax.ShapeDtypeStruct((TOK * HD, NOPE + ROPE), F32),
            jax.ShapeDtypeStruct((36, TOK), F32),
            jax.ShapeDtypeStruct((64, KVD), F32),
        ),
        in_specs=[pl.BlockSpec(memory_space=pltpu.HBM)] * 5,
        out_specs=[pl.BlockSpec(memory_space=pltpu.VMEM)] * 3,
        scratch_shapes=[
            vm((TOK * HD, NOPE + ROPE), BF16),
            vm((TOK * HD, VDIM), BF16),
            vm((LAT * HD, KVD), BF16),
            vm((32, 128), jnp.int32),
            vm((WIN, LAT + ROPE), BF16),
            vm((2, LAT, 128), F32),
            vm((HD, LAT, KVD), BF16),
            vm((2, TOK * HD, 128), F32),
            vm((TOK * HD, VDIM), F32),
            vm((2, TOK * HD, 128), F32),
            vm((HD, WIN, KVD), BF16),
            vm((HD, WIN, KVD), BF16),
            vm((HD * TOK, WIN), BF16),
            vm((HD * TOK, 128), BF16),
            vm((LAT + ROPE, WIN), F32),
            vm((LAT + ROPE, WIN), BF16),
            vm((2, L, L, 16, 512), BF16),
            vm((4, 10, 2, 16, 512), BF16),
            vm((4, L, 16, 512), BF16),
            vm((2, L, 16, 512), BF16),
            vm((NH, KROWS, WIN), BF16),
            vm((KROWS, WIN), F32),
            vm((KROWS, WIN), F32),
            vm((2, 16, 512), F32),
            vm((2, 64, 128), F32),
            pltpu.SemaphoreType.REGULAR,
            pltpu.SemaphoreType.REGULAR,
            dma((5,)),
            dma((2,)),
            dma((4, len(STEPS))),
            dma((4, len(STEPS))),
            dma((2, L)),
            dma((2, L)),
            dma((NH,)),
            dma((NH,)),
            dma((2,)),
        ],
        compiler_params=pltpu.CompilerParams(
            collective_id=0, has_side_effects=True, vmem_limit_bytes=32 * 1024 * 1024
        ),
        name="mla_backward",
    )(
        *(
            pltpu.with_memory_space_constraint(a, pltpu.HBM)
            for a in (
                queries.reshape(TOK * HD, NOPE + ROPE),
                latent_keys,
                out_grad.reshape(TOK * HD, VDIM),
                up_weight.reshape(LAT * HD, KVD),
                segment_ids.reshape(32, 128),
            )
        )
    )
    dq, kg, wg = pl.pallas_call(
        hand_out,
        out_shape=tuple(jax.ShapeDtypeStruct(a.shape, a.dtype) for a in (dq, kg, wg)),
        in_specs=[pl.BlockSpec(memory_space=pl.ANY)] * 3,
        out_specs=[pl.BlockSpec(memory_space=pl.ANY)] * 3,
        scratch_shapes=[dma((3,))],
        compiler_params=pltpu.CompilerParams(vmem_limit_bytes=8 * 1024 * 1024),
        name="hand_out",
    )(dq, kg, wg)
    return (
        dq.reshape(TOK, HD, NOPE + ROPE),
        kg.T,
        wg.reshape(8, HD, KVD),
    )


def solution(mesh):
    return jax.shard_map(
        shards,
        mesh=mesh,
        in_specs=(
            P("ctx", "head", None),
            P("ctx", None),
            P("ctx", "head", None),
            P(None, "head", None),
            P(),
        ),
        out_specs=(P("ctx", "head", None), P("ctx", "head"), P("ctx", "head", None)),
        check_vma=False,
    )
```

```python
import math

import jax
import jax.numpy as jnp
from jax import lax
from jax.experimental import pallas as pl
from jax.experimental.pallas import tpu as pltpu
from jax.sharding import PartitionSpec as P

LAT = 512
ROPE = 64
NOPE = 128
VDIM = 128
KVD = NOPE + VDIM
TOK = 64
WIN = 128
HD = 8
L = 8
NH = 16
KROWS = 48
MESH = pl.DeviceIdType.MESH
F32 = jnp.float32
BF16 = jnp.bfloat16

STEPS = (
    (4, 0), (4, 1), (3, 2), (3, 3), (3, 0), (3, 1), (2, 2),
    (2, 3), (2, 0), (2, 1), (1, 2), (1, 3), (1, 0), (1, 1),
)
LAG = 4


def dot(a, b, ca, cb):
    return lax.dot_general(a, b, (((ca,), (cb,)), ((), ())), preferred_element_type=F32)


def kernel(
    q_hbm, lat_hbm, do_hbm, w_hbm, seg_hbm,
    dq_v, kg_v, wg_v,
    q_v, do_v, w_v, seg_v, latwin,
    wf, wflat, qf, dof, dqf,
    kv_v, dkv_v, ds_v, qr_v, kt32, kt16,
    term, ring, fin, part, kr, kpart, kprev, wgf, wgs,
    plane_sem, z_sem, in_sem, halo_sem, ring_send, ring_recv, p2_send, p2_recv, k_send, k_recv, kp_sem,
):
    c = lax.axis_index("ctx")
    h = lax.axis_index("head")
    y = lax.div(c, L)
    x = lax.rem(c, L)
    nxt = lax.rem(c + 1, L * L)
    prv = lax.rem(c + L * L - 1, L * L)

    def ctx_of(yy, xx):
        return yy * L + xx

    lat_cp = pltpu.make_async_copy(lat_hbm, latwin.at[pl.ds(TOK, TOK)], in_sem.at[0])
    w_cp = pltpu.make_async_copy(w_hbm, w_v, in_sem.at[1])
    q_cp = pltpu.make_async_copy(q_hbm, q_v, in_sem.at[2])
    do_cp = pltpu.make_async_copy(do_hbm, do_v, in_sem.at[3])
    seg_cp = pltpu.make_async_copy(seg_hbm, seg_v, in_sem.at[4])
    for cp in (lat_cp, q_cp, do_cp, seg_cp, w_cp):
        cp.start()

    core = lax.rem(h, 2)
    z = lax.div(h, 2)
    chip0, chip1 = (c, 2 * z), (c, 2 * z + 1)
    barrier = pltpu.get_barrier_semaphore()
    near = [nxt, prv]
    for d in (1, L - 1):
        near += [ctx_of(y, lax.rem(x + d, L)), ctx_of(lax.rem(y + d, L), x)]
    for to in near:
        pl.semaphore_signal(barrier, inc=1, device_id=(to, 2 * z), device_id_type=MESH)

    @pl.when(core == 1)
    def _():
        pl.semaphore_signal(barrier, inc=1, device_id=chip0, device_id_type=MESH)

    for d in range(1, NH // 2):
        pl.semaphore_signal(
            barrier,
            inc=1,
            device_id=(c, 2 * lax.rem(z + d, NH // 2) + 1),
            device_id_type=MESH,
        )

    lat_cp.wait()

    @pl.when(core == 0)
    def _():
        pl.semaphore_wait(barrier, 2 * len(near) + 1)
        pl.semaphore_signal(plane_sem, inc=1, device_id=chip1, device_id_type=MESH)

    @pl.when(core == 1)
    def _():
        pl.semaphore_wait(plane_sem, 1)

    halo = pltpu.make_async_remote_copy(
        src_ref=latwin.at[pl.ds(TOK, TOK)],
        dst_ref=latwin.at[pl.ds(0, TOK)],
        send_sem=halo_sem.at[0],
        recv_sem=halo_sem.at[1],
        device_id=(nxt, h),
        device_id_type=MESH,
    )
    first, final = c == 0, c == L * L - 1

    @pl.when(jnp.logical_not(final))
    def _():
        halo.start()

    @pl.when(first)
    def _():
        latwin[:TOK, :] = jnp.zeros((TOK, LAT + ROPE), BF16)

    q_cp.wait()
    do_cp.wait()
    qf[1] = jnp.zeros((TOK * HD, 128), F32)
    qf[0] = q_v[:, :NOPE].astype(F32)
    qf[1, :, :ROPE] = q_v[:, NOPE:].astype(F32)
    dof[...] = do_v[...].astype(F32)
    qn, dob = [], []
    for hd in range(HD):
        qn.append(qf[0, pl.ds(hd, TOK, stride=HD), :].astype(BF16))
        qr_v[pl.ds(hd * TOK, TOK), :] = qf[1, pl.ds(hd, TOK, stride=HD), :].astype(BF16)
        dob.append(dof[pl.ds(hd, TOK, stride=HD), :].astype(BF16))

    w_cp.wait()
    rows = LAT * HD // 8

    def relayout(i, carry):
        base = pl.multiple_of(i * rows, rows)
        out = pl.multiple_of(i * (LAT // 8), LAT // 8)
        for half in range(2):
            wf[half] = w_v[pl.ds(base, rows), half * 128 : (half + 1) * 128].astype(F32)
        for hd in range(HD):
            for half in range(2):
                wflat[hd, pl.ds(out, LAT // 8), half * 128 : (half + 1) * 128] = wf[
                    half, pl.ds(hd, LAT // 8, stride=HD), :
                ].astype(BF16)
        return carry

    lax.fori_loop(0, 8, relayout, 0)

    seg_cp.wait()
    row = lax.div(c, 2)
    odd = lax.rem(c, 2)
    lane = lax.broadcasted_iota(jnp.int32, (1, WIN), 1)
    row_a = seg_v[pl.ds(row, 1), :]
    row_b = seg_v[pl.ds(jnp.maximum(row - 1, 0), 1), :]
    mixed = pltpu.roll(jnp.where(lane >= TOK, row_b, row_a), TOK, 1)
    seg_row = jnp.where(odd == 1, row_a, mixed)
    seg_row = jnp.where((lane < TOK) & (c == 0), -1, seg_row).astype(F32)
    seg_all = jnp.broadcast_to(seg_row, (WIN, WIN))
    seg_col = seg_all.T[TOK:, :]
    seg_all = seg_all[:TOK, :]
    pos_key = lax.broadcasted_iota(jnp.int32, (TOK, WIN), 1)
    pos_query = lax.broadcasted_iota(jnp.int32, (TOK, WIN), 0) + TOK
    visible = (seg_col == seg_all) & (pos_key <= pos_query)

    for hd in range(HD):
        kv_v[hd, TOK:, :] = dot(latwin[TOK:, :LAT], wflat[hd], 1, 0).astype(BF16)

    @pl.when(jnp.logical_not(first))
    def _():
        halo.wait_recv()

    for hd in range(HD):
        kv_v[hd, :TOK, :] = dot(latwin[:TOK, :LAT], wflat[hd], 1, 0).astype(BF16)

    k_rope = jnp.concatenate([latwin[:, LAT:], jnp.zeros((WIN, 128 - ROPE), BF16)], 1)
    scale = 1.0 / math.sqrt(NOPE + ROPE)
    scores, dprobs = [], []
    for hd in range(HD):
        key = kv_v[hd, :, :NOPE]
        val = kv_v[hd, :, NOPE:]
        q_rope = qr_v[pl.ds(hd * TOK, TOK), :]
        scores.append(dot(qn[hd], key, 1, 1) + dot(q_rope, k_rope, 1, 1))
        dprobs.append(dot(dob[hd], val, 1, 1))
    for hd in range(HD):
        s = jnp.where(visible, scores[hd] * scale, -1e30)
        top = jnp.max(s, -1, keepdims=True)
        expo = jnp.where(visible, jnp.exp(s - top), 0.0)
        probs = expo / jnp.sum(expo, -1, keepdims=True)
        delta = jnp.sum(probs * dprobs[hd], -1, keepdims=True)
        ds = (probs * (dprobs[hd] - delta) * scale).astype(BF16)
        p16 = probs.astype(BF16)
        ds_v[pl.ds(hd * TOK, TOK), :] = ds
        dkv_v[hd, :, :NOPE] = dot(ds, qn[hd], 0, 0).astype(BF16)
        dkv_v[hd, :, NOPE:] = dot(p16, dob[hd], 0, 0).astype(BF16)

    lat_t = latwin[:, :LAT].T

    def terms(part_id):
        for side in range(2):
            a = 4 * part_id + side
            lo = dot(lat_t, dkv_v[a], 1, 0).reshape(L * L, 8, KVD)
            hi = dot(lat_t, dkv_v[a + 2], 1, 0).reshape(L * L, 8, KVD)
            both = jnp.concatenate([lo, hi], 1).astype(BF16).reshape(L, L, 16, KVD)
            for i in range(L):
                block = both[:, i] if part_id == 0 else both[i]
                term[part_id, i, :, :, side * KVD : (side + 1) * KVD] = block

    def place(part_id, sign, dist):
        pos = x if part_id == 0 else y
        return lax.rem(pos + sign * dist + L, L)

    def neighbour(part_id, sign):
        if part_id == 0:
            return (ctx_of(y, lax.rem(x + sign + L, L)), h)
        return (ctx_of(lax.rem(y + sign + L, L), x), h)

    def message(g, m):
        part_id, back = g // 2, g % 2
        sign = -1 if back else 1
        dist, quarter = STEPS[m]
        quarter = quarter ^ (2 * back)
        src = term.at[part_id, place(part_id, sign, dist), pl.ds(2 * quarter, 2)]
        dst = fin.at[g, pl.ds(2 * quarter, 2)] if dist == 1 else ring.at[g, m]
        return pltpu.make_async_remote_copy(
            src_ref=src,
            dst_ref=dst,
            send_sem=ring_send.at[g, m],
            recv_sem=ring_recv.at[g, m],
            device_id=neighbour(part_id, sign),
            device_id_type=MESH,
        )

    def add(g, m):
        part_id, back = g // 2, g % 2
        sign = -1 if back else 1
        dist, quarter = STEPS[m]
        quarter = quarter ^ (2 * back)
        at = place(part_id, sign, dist)
        own = term[part_id, at, pl.ds(2 * quarter, 2)].astype(F32)
        term[part_id, at, pl.ds(2 * quarter, 2)] = (own + ring[g, m - LAG].astype(F32)).astype(
            BF16
        )

    def advance(lo, hi, directions=range(4)):
        for m in range(lo, hi):
            for g in directions:
                message(g, m - LAG).wait_recv()
                add(g, m)
                message(g, m).start()

    for part_id in range(2):
        terms(part_id)
        for g in (2 * part_id, 2 * part_id + 1):
            for m in range(LAG):
                message(g, m).start()

    acc = dot(wflat[0], dkv_v[0], 1, 1)
    for hd in range(1, HD):
        acc = acc + dot(wflat[hd], dkv_v[hd], 1, 1)
    kt32[pl.ds(0, LAT), :] = acc
    kt32[pl.ds(LAT, ROPE), :] = dot(qr_v[...], ds_v[...], 0, 0)[:ROPE, :]
    kt16[...] = kt32[...].astype(BF16)

    def k_start(to):
        return pl.multiple_of(lax.div(36 * to, 16) * 16, 16)

    def k_copy(d):
        to = lax.rem(h + d, NH)
        return pltpu.make_async_remote_copy(
            src_ref=kt16.at[pl.ds(k_start(to), KROWS)],
            dst_ref=kr.at[d],
            send_sem=k_send.at[d],
            recv_sem=k_recv.at[d],
            device_id=(c, to),
            device_id_type=MESH,
        )

    def k_exchange():
        @pl.when(core == 1)
        def _():
            pl.semaphore_wait(barrier, NH - 2)
            pl.semaphore_signal(z_sem, inc=1, device_id=chip0, device_id_type=MESH)

        @pl.when(core == 0)
        def _():
            pl.semaphore_wait(z_sem, 1)

        for d in range(1, NH):
            k_copy(d).start()

    pl.when(z >= 4)(k_exchange)

    for hd in range(HD):
        ds = ds_v[pl.ds(hd * TOK, TOK), :]
        dqf[0, pl.ds(hd, TOK, stride=HD), :] = dot(ds, kv_v[hd, :, :NOPE], 1, 0)
        dqf[1, pl.ds(hd, TOK, stride=HD), :] = dot(ds, k_rope, 1, 0)
    dq_v[:, :NOPE] = dqf[0]
    dq_v[:, NOPE:] = dqf[1, :, :ROPE]

    row0 = (h == 0) & (y == 0) & (x > 0)
    col0 = (h == 0) & (x == 0) & (y > 0)

    def in_turn(first_part):
        own = (2 * first_part, 2 * first_part + 1)
        rest = (2 - 2 * first_part, 3 - 2 * first_part)
        advance(LAG, len(STEPS), own)
        advance(LAG, 10, rest)
        k_exchange()
        advance(10, len(STEPS), rest)

    @pl.when(row0)
    def _():
        in_turn(1)

    @pl.when(col0)
    def _():
        in_turn(0)

    @pl.when(jnp.logical_not(row0 | col0))
    def _():
        advance(LAG, 10)
        pl.when(z < 4)(k_exchange)
        advance(10, len(STEPS))

    def p2(part_id, to, frm):
        dev = (ctx_of(to, x), h) if part_id == 0 else (ctx_of(y, to), h)
        return pltpu.make_async_remote_copy(
            src_ref=term.at[part_id, x if part_id == 0 else y, to],
            dst_ref=part.at[part_id, frm],
            send_sem=p2_send.at[part_id, to],
            recv_sem=p2_recv.at[part_id, frm],
            device_id=dev,
            device_id_type=MESH,
        )

    def finish(part_id, quarter):
        mine = x if part_id == 0 else y
        pos = y if part_id == 0 else x
        at = pl.ds(2 * quarter, 2)
        summed = (
            term[part_id, mine, at].astype(F32)
            + fin[2 * part_id, at].astype(F32)
            + fin[2 * part_id + 1, at].astype(F32)
        )
        term[part_id, mine, at] = summed.astype(BF16)
        for j in range(2):
            to = 2 * quarter + j

            @pl.when(pos == to)
            def _():
                wgf[part_id] = summed[j]

            @pl.when(pos != to)
            def _():
                p2(part_id, to, pos).start()

    for last in range(2):
        for g in range(4):
            message(g, 10 + last).wait_recv()
            message(g, 12 + last).wait_recv()
        for part_id in range(2):
            finish(part_id, last)
            finish(part_id, 2 + last)

    total = kt32[pl.ds(k_start(h), KROWS), :]
    for d in range(1, NH):
        k_copy(d).wait_recv()
        total = total + kr[d].astype(F32)
    kpart[...] = total
    kp = pltpu.make_async_remote_copy(
        src_ref=kpart,
        dst_ref=kprev,
        send_sem=kp_sem.at[0],
        recv_sem=kp_sem.at[1],
        device_id=(prv, h),
        device_id_type=MESH,
    )

    @pl.when(jnp.logical_not(first))
    def _():
        kp.start()

    for part_id in range(2):
        pos = y if part_id == 0 else x
        total = wgf[part_id]
        for d in range(1, L):
            frm = lax.rem(pos + d, L)
            p2(part_id, frm, frm).wait_recv()
            total = total + part[part_id, frm].astype(F32)
        for a in range(4):
            rows0 = (a // 2) * 8
            for half in range(2):
                cols = (a % 2) * KVD + half * 128
                wgs[half, pl.ds(4 * part_id + a, 8, stride=HD), :] = total[
                    rows0 : rows0 + 8, cols : cols + 128
                ]
    wg_v[:, :128] = wgs[0]
    wg_v[:, 128:] = wgs[1]

    @pl.when(jnp.logical_not(final))
    def _():
        kp.wait_recv()

    @pl.when(final)
    def _():
        kprev[...] = jnp.zeros((KROWS, WIN), F32)

    both = pltpu.roll(kpart[...], TOK, 1) + kprev[...]
    off = lax.rem(36 * h, 16)
    pick = both
    for o in (4, 8, 12):
        pick = jnp.where(off == o, pltpu.roll(both, KROWS - o, 0), pick)
    kg_v[...] = pick[:36, :TOK]

    @pl.when(jnp.logical_not(final))
    def _():
        halo.wait_send()

    @pl.when(jnp.logical_not(first))
    def _():
        kp.wait_send()

    for d in range(1, NH):
        k_copy(d).wait_send()
    for g in range(4):
        for m in range(len(STEPS)):
            message(g, m).wait_send()
    for part_id in range(2):
        pos = y if part_id == 0 else x
        for d in range(1, L):
            p2(part_id, lax.rem(pos + d, L), pos).wait_send()


def hand_out(dq, kg, wg, dq_to, kg_to, wg_to, sem):
    copies = [
        pltpu.make_async_copy(src, dst, sem.at[i])
        for i, (src, dst) in enumerate(((dq, dq_to), (kg, kg_to), (wg, wg_to)))
    ]
    for cp in copies:
        cp.start()
    for cp in copies:
        cp.wait()


def shards(queries, latent_keys, out_grad, up_weight, segment_ids):
    vm, dma = pltpu.VMEM, pltpu.SemaphoreType.DMA
    dq, kg, wg = pl.pallas_call(
        kernel,
        out_shape=(
            jax.ShapeDtypeStruct((TOK * HD, NOPE + ROPE), F32),
            jax.ShapeDtypeStruct((36, TOK), F32),
            jax.ShapeDtypeStruct((64, KVD), F32),
        ),
        in_specs=[pl.BlockSpec(memory_space=pltpu.HBM)] * 5,
        out_specs=[pl.BlockSpec(memory_space=pltpu.VMEM)] * 3,
        scratch_shapes=[
            vm((TOK * HD, NOPE + ROPE), BF16),
            vm((TOK * HD, VDIM), BF16),
            vm((LAT * HD, KVD), BF16),
            vm((32, 128), jnp.int32),
            vm((WIN, LAT + ROPE), BF16),
            vm((2, LAT, 128), F32),
            vm((HD, LAT, KVD), BF16),
            vm((2, TOK * HD, 128), F32),
            vm((TOK * HD, VDIM), F32),
            vm((2, TOK * HD, 128), F32),
            vm((HD, WIN, KVD), BF16),
            vm((HD, WIN, KVD), BF16),
            vm((HD * TOK, WIN), BF16),
            vm((HD * TOK, 128), BF16),
            vm((LAT + ROPE, WIN), F32),
            vm((LAT + ROPE, WIN), BF16),
            vm((2, L, L, 16, 512), BF16),
            vm((4, 10, 2, 16, 512), BF16),
            vm((4, L, 16, 512), BF16),
            vm((2, L, 16, 512), BF16),
            vm((NH, KROWS, WIN), BF16),
            vm((KROWS, WIN), F32),
            vm((KROWS, WIN), F32),
            vm((2, 16, 512), F32),
            vm((2, 64, 128), F32),
            pltpu.SemaphoreType.REGULAR,
            pltpu.SemaphoreType.REGULAR,
            dma((5,)),
            dma((2,)),
            dma((4, len(STEPS))),
            dma((4, len(STEPS))),
            dma((2, L)),
            dma((2, L)),
            dma((NH,)),
            dma((NH,)),
            dma((2,)),
        ],
        compiler_params=pltpu.CompilerParams(
            collective_id=0, has_side_effects=True, vmem_limit_bytes=32 * 1024 * 1024
        ),
        name="mla_backward",
    )(
        *(
            pltpu.with_memory_space_constraint(a, pltpu.HBM)
            for a in (
                queries.reshape(TOK * HD, NOPE + ROPE),
                latent_keys,
                out_grad.reshape(TOK * HD, VDIM),
                up_weight.reshape(LAT * HD, KVD),
                segment_ids.reshape(32, 128),
            )
        )
    )
    dq, kg, wg = pl.pallas_call(
        hand_out,
        out_shape=tuple(jax.ShapeDtypeStruct(a.shape, a.dtype) for a in (dq, kg, wg)),
        in_specs=[pl.BlockSpec(memory_space=pl.ANY)] * 3,
        out_specs=[pl.BlockSpec(memory_space=pl.ANY)] * 3,
        scratch_shapes=[dma((3,))],
        compiler_params=pltpu.CompilerParams(vmem_limit_bytes=8 * 1024 * 1024),
        name="hand_out",
    )(dq, kg, wg)
    return (
        dq.reshape(TOK, HD, NOPE + ROPE),
        kg.T,
        wg.reshape(8, HD, KVD),
    )


def solution(mesh):
    return jax.shard_map(
        shards,
        mesh=mesh,
        in_specs=(
            P("ctx", "head", None),
            P("ctx", None),
            P("ctx", "head", None),
            P(None, "head", None),
            P(),
        ),
        out_specs=(P("ctx", "head", None), P("ctx", "head"), P("ctx", "head", None)),
        check_vma=False,
    )
```

```python
import math

import jax
import jax.numpy as jnp
from jax import lax
from jax.experimental import pallas as pl
from jax.experimental.pallas import tpu as pltpu
from jax.sharding import PartitionSpec as P

LAT = 512
ROPE = 64
NOPE = 128
VDIM = 128
KVD = NOPE + VDIM
TOK = 64
WIN = 128
HD = 8
L = 8
NH = 16
KROWS = 48
MESH = pl.DeviceIdType.MESH
F32 = jnp.float32
BF16 = jnp.bfloat16

STEPS = (
    (4, 0), (4, 1), (3, 2), (3, 3), (3, 0), (3, 1), (2, 2),
    (2, 3), (2, 0), (2, 1), (1, 2), (1, 3), (1, 0), (1, 1),
)
LAG = 4


def dot(a, b, ca, cb):
    return lax.dot_general(a, b, (((ca,), (cb,)), ((), ())), preferred_element_type=F32)


def kernel(
    q_hbm, lat_hbm, do_hbm, w_hbm, seg_hbm,
    dq_v, kg_v, wg_v,
    q_v, do_v, w_v, seg_v, latwin,
    wf, wflat, qf, dof, dqf,
    kv_v, dkv_v, ds_v, qr_v, kt32, kt16,
    term, ring, fin, part, kr, kpart, kprev, wgf, wgs,
    plane_sem, z_sem, in_sem, halo_sem, ring_send, ring_recv, p2_send, p2_recv, k_send, k_recv, kp_sem,
):
    c = lax.axis_index("ctx")
    h = lax.axis_index("head")
    y = lax.div(c, L)
    x = lax.rem(c, L)
    nxt = lax.rem(c + 1, L * L)
    prv = lax.rem(c + L * L - 1, L * L)

    def ctx_of(yy, xx):
        return yy * L + xx

    lat_cp = pltpu.make_async_copy(lat_hbm, latwin.at[pl.ds(TOK, TOK)], in_sem.at[0])
    w_cp = pltpu.make_async_copy(w_hbm, w_v, in_sem.at[1])
    q_cp = pltpu.make_async_copy(q_hbm, q_v, in_sem.at[2])
    do_cp = pltpu.make_async_copy(do_hbm, do_v, in_sem.at[3])
    seg_cp = pltpu.make_async_copy(seg_hbm, seg_v, in_sem.at[4])
    for cp in (lat_cp, q_cp, do_cp, seg_cp, w_cp):
        cp.start()

    odd_x = lax.rem(c, 2)
    even_ctx = c - odd_x
    odd_ctx = even_ctx + 1
    z = lax.div(h, 2)
    barrier = pltpu.get_barrier_semaphore()

    def greet(to):
        gate = to - lax.rem(to, 2)

        @pl.when(gate != c)
        def _():
            pl.semaphore_signal(barrier, inc=1, device_id=(gate, h), device_id_type=MESH)

    greet(nxt)
    greet(prv)
    for d in (1, L - 1):
        greet(ctx_of(y, lax.rem(x + d, L)))
        greet(ctx_of(lax.rem(y + d, L), x))
    for d in range(1, NH):
        pl.semaphore_signal(
            barrier, inc=1, device_id=(odd_ctx, lax.rem(h + d, NH)), device_id_type=MESH
        )

    lat_cp.wait()

    @pl.when(odd_x == 0)
    def _():
        pl.semaphore_wait(barrier, 10)
        pl.semaphore_signal(plane_sem, inc=1, device_id=(odd_ctx, h), device_id_type=MESH)

    @pl.when(odd_x == 1)
    def _():
        pl.semaphore_wait(plane_sem, 1)

    halo = pltpu.make_async_remote_copy(
        src_ref=latwin.at[pl.ds(TOK, TOK)],
        dst_ref=latwin.at[pl.ds(0, TOK)],
        send_sem=halo_sem.at[0],
        recv_sem=halo_sem.at[1],
        device_id=(nxt, h),
        device_id_type=MESH,
    )
    first, final = c == 0, c == L * L - 1

    @pl.when(jnp.logical_not(final))
    def _():
        halo.start()

    @pl.when(first)
    def _():
        latwin[:TOK, :] = jnp.zeros((TOK, LAT + ROPE), BF16)

    q_cp.wait()
    do_cp.wait()
    qf[1] = jnp.zeros((TOK * HD, 128), F32)
    qf[0] = q_v[:, :NOPE].astype(F32)
    qf[1, :, :ROPE] = q_v[:, NOPE:].astype(F32)
    dof[...] = do_v[...].astype(F32)
    qn, dob = [], []
    for hd in range(HD):
        qn.append(qf[0, pl.ds(hd, TOK, stride=HD), :].astype(BF16))
        qr_v[pl.ds(hd * TOK, TOK), :] = qf[1, pl.ds(hd, TOK, stride=HD), :].astype(BF16)
        dob.append(dof[pl.ds(hd, TOK, stride=HD), :].astype(BF16))

    w_cp.wait()
    rows = LAT * HD // 8

    def relayout(i, carry):
        base = pl.multiple_of(i * rows, rows)
        out = pl.multiple_of(i * (LAT // 8), LAT // 8)
        for half in range(2):
            wf[half] = w_v[pl.ds(base, rows), half * 128 : (half + 1) * 128].astype(F32)
        for hd in range(HD):
            for half in range(2):
                wflat[hd, pl.ds(out, LAT // 8), half * 128 : (half + 1) * 128] = wf[
                    half, pl.ds(hd, LAT // 8, stride=HD), :
                ].astype(BF16)
        return carry

    lax.fori_loop(0, 8, relayout, 0)

    seg_cp.wait()
    row = lax.div(c, 2)
    odd = lax.rem(c, 2)
    lane = lax.broadcasted_iota(jnp.int32, (1, WIN), 1)
    row_a = seg_v[pl.ds(row, 1), :]
    row_b = seg_v[pl.ds(jnp.maximum(row - 1, 0), 1), :]
    mixed = pltpu.roll(jnp.where(lane >= TOK, row_b, row_a), TOK, 1)
    seg_row = jnp.where(odd == 1, row_a, mixed)
    seg_row = jnp.where((lane < TOK) & (c == 0), -1, seg_row).astype(F32)
    seg_all = jnp.broadcast_to(seg_row, (WIN, WIN))
    seg_col = seg_all.T[TOK:, :]
    seg_all = seg_all[:TOK, :]
    pos_key = lax.broadcasted_iota(jnp.int32, (TOK, WIN), 1)
    pos_query = lax.broadcasted_iota(jnp.int32, (TOK, WIN), 0) + TOK
    visible = (seg_col == seg_all) & (pos_key <= pos_query)

    for hd in range(HD):
        kv_v[hd, TOK:, :] = dot(latwin[TOK:, :LAT], wflat[hd], 1, 0).astype(BF16)

    @pl.when(jnp.logical_not(first))
    def _():
        halo.wait_recv()

    for hd in range(HD):
        kv_v[hd, :TOK, :] = dot(latwin[:TOK, :LAT], wflat[hd], 1, 0).astype(BF16)

    k_rope = jnp.concatenate([latwin[:, LAT:], jnp.zeros((WIN, 128 - ROPE), BF16)], 1)
    scale = 1.0 / math.sqrt(NOPE + ROPE)
    scores, dprobs = [], []
    s_rope = dot(qr_v[...], k_rope, 1, 1)
    for hd in range(HD):
        key = kv_v[hd, :, :NOPE]
        val = kv_v[hd, :, NOPE:]
        scores.append(dot(qn[hd], key, 1, 1) + s_rope[hd * TOK : (hd + 1) * TOK])
        dprobs.append(dot(dob[hd], val, 1, 1))
    for hd in range(HD):
        s = jnp.where(visible, scores[hd] * scale, -1e30)
        top = jnp.max(s, -1, keepdims=True)
        expo = jnp.where(visible, jnp.exp(s - top), 0.0)
        probs = expo / jnp.sum(expo, -1, keepdims=True)
        delta = jnp.sum(probs * dprobs[hd], -1, keepdims=True)
        ds = (probs * (dprobs[hd] - delta) * scale).astype(BF16)
        p16 = probs.astype(BF16)
        ds_v[pl.ds(hd * TOK, TOK), :] = ds
        dkv_v[hd, :, :NOPE] = dot(ds, qn[hd], 0, 0).astype(BF16)
        dkv_v[hd, :, NOPE:] = dot(p16, dob[hd], 0, 0).astype(BF16)

    lat_t = latwin[:, :LAT].T

    def terms(part_id):
        for side in range(2):
            a = 4 * part_id + side
            lo = dot(lat_t, dkv_v[a], 1, 0).reshape(L * L, 8, KVD)
            hi = dot(lat_t, dkv_v[a + 2], 1, 0).reshape(L * L, 8, KVD)
            both = jnp.concatenate([lo, hi], 1).astype(BF16).reshape(L, L, 16, KVD)
            for i in range(L):
                block = both[:, i] if part_id == 0 else both[i]
                term[part_id, i, :, :, side * KVD : (side + 1) * KVD] = block

    def place(part_id, sign, dist):
        pos = x if part_id == 0 else y
        return lax.rem(pos + sign * dist + L, L)

    def neighbour(part_id, sign):
        if part_id == 0:
            return (ctx_of(y, lax.rem(x + sign + L, L)), h)
        return (ctx_of(lax.rem(y + sign + L, L), x), h)

    def message(g, m):
        part_id, back = g // 2, g % 2
        sign = -1 if back else 1
        dist, quarter = STEPS[m]
        quarter = quarter ^ (2 * back)
        src = term.at[part_id, place(part_id, sign, dist), pl.ds(2 * quarter, 2)]
        dst = fin.at[g, pl.ds(2 * quarter, 2)] if dist == 1 else ring.at[g, m]
        return pltpu.make_async_remote_copy(
            src_ref=src,
            dst_ref=dst,
            send_sem=ring_send.at[g, m],
            recv_sem=ring_recv.at[g, m],
            device_id=neighbour(part_id, sign),
            device_id_type=MESH,
        )

    def add(g, m):
        part_id, back = g // 2, g % 2
        sign = -1 if back else 1
        dist, quarter = STEPS[m]
        quarter = quarter ^ (2 * back)
        at = place(part_id, sign, dist)
        own = term[part_id, at, pl.ds(2 * quarter, 2)].astype(F32)
        term[part_id, at, pl.ds(2 * quarter, 2)] = (own + ring[g, m - LAG].astype(F32)).astype(
            BF16
        )

    def advance(lo, hi):
        for m in range(lo, hi):
            for g in range(4):
                message(g, m - LAG).wait_recv()
                add(g, m)
                message(g, m).start()

    for part_id in range(2):
        terms(part_id)
        for g in (2 * part_id, 2 * part_id + 1):
            for m in range(LAG):
                message(g, m).start()

    acc = dot(wflat[0], dkv_v[0], 1, 1)
    for hd in range(1, HD):
        acc = acc + dot(wflat[hd], dkv_v[hd], 1, 1)
    kt32[pl.ds(0, LAT), :] = acc
    kt32[pl.ds(LAT, ROPE), :] = dot(qr_v[...], ds_v[...], 0, 0)[:ROPE, :]
    kt16[...] = kt32[...].astype(BF16)

    def k_start(to):
        return pl.multiple_of(lax.div(36 * to, 16) * 16, 16)

    def k_copy(d):
        to = lax.rem(h + d, NH)
        return pltpu.make_async_remote_copy(
            src_ref=kt16.at[pl.ds(k_start(to), KROWS)],
            dst_ref=kr.at[d],
            send_sem=k_send.at[d],
            recv_sem=k_recv.at[d],
            device_id=(c, to),
            device_id_type=MESH,
        )

    def k_exchange():
        @pl.when(odd_x == 1)
        def _():
            pl.semaphore_wait(barrier, 2 * (NH - 1))
            pl.semaphore_signal(z_sem, inc=1, device_id=(even_ctx, h), device_id_type=MESH)

        @pl.when(odd_x == 0)
        def _():
            pl.semaphore_wait(z_sem, 1)

        for d in range(1, NH):
            k_copy(d).start()

    pl.when(z >= 4)(k_exchange)

    for hd in range(HD):
        ds = ds_v[pl.ds(hd * TOK, TOK), :]
        dqf[0, pl.ds(hd, TOK, stride=HD), :] = dot(ds, kv_v[hd, :, :NOPE], 1, 0)
        dqf[1, pl.ds(hd, TOK, stride=HD), :] = dot(ds, k_rope, 1, 0)
    dq_v[:, :NOPE] = dqf[0]
    dq_v[:, NOPE:] = dqf[1, :, :ROPE]

    advance(LAG, 10)
    pl.when(z < 4)(k_exchange)
    advance(10, len(STEPS))

    def p2(part_id, to, frm):
        dev = (ctx_of(to, x), h) if part_id == 0 else (ctx_of(y, to), h)
        return pltpu.make_async_remote_copy(
            src_ref=term.at[part_id, x if part_id == 0 else y, to],
            dst_ref=part.at[part_id, frm],
            send_sem=p2_send.at[part_id, to],
            recv_sem=p2_recv.at[part_id, frm],
            device_id=dev,
            device_id_type=MESH,
        )

    def finish(part_id, quarter):
        mine = x if part_id == 0 else y
        pos = y if part_id == 0 else x
        at = pl.ds(2 * quarter, 2)
        summed = (
            term[part_id, mine, at].astype(F32)
            + fin[2 * part_id, at].astype(F32)
            + fin[2 * part_id + 1, at].astype(F32)
        )
        term[part_id, mine, at] = summed.astype(BF16)
        for j in range(2):
            to = 2 * quarter + j

            @pl.when(pos == to)
            def _():
                wgf[part_id] = summed[j]

            @pl.when(pos != to)
            def _():
                p2(part_id, to, pos).start()

    for last in range(2):
        for g in range(4):
            message(g, 10 + last).wait_recv()
            message(g, 12 + last).wait_recv()
        for part_id in range(2):
            finish(part_id, last)
            finish(part_id, 2 + last)

    total = kt32[pl.ds(k_start(h), KROWS), :]
    for d in range(1, NH):
        k_copy(d).wait_recv()
        total = total + kr[d].astype(F32)
    kpart[...] = total
    kp = pltpu.make_async_remote_copy(
        src_ref=kpart,
        dst_ref=kprev,
        send_sem=kp_sem.at[0],
        recv_sem=kp_sem.at[1],
        device_id=(prv, h),
        device_id_type=MESH,
    )

    @pl.when(jnp.logical_not(first))
    def _():
        kp.start()

    for part_id in range(2):
        pos = y if part_id == 0 else x
        total = wgf[part_id]
        for d in range(1, L):
            frm = lax.rem(pos + d, L)
            p2(part_id, frm, frm).wait_recv()
            total = total + part[part_id, frm].astype(F32)
        for a in range(4):
            rows0 = (a // 2) * 8
            for half in range(2):
                cols = (a % 2) * KVD + half * 128
                wgs[half, pl.ds(4 * part_id + a, 8, stride=HD), :] = total[
                    rows0 : rows0 + 8, cols : cols + 128
                ]
    wg_v[:, :128] = wgs[0]
    wg_v[:, 128:] = wgs[1]

    @pl.when(jnp.logical_not(final))
    def _():
        kp.wait_recv()

    @pl.when(final)
    def _():
        kprev[...] = jnp.zeros((KROWS, WIN), F32)

    both = pltpu.roll(kpart[...], TOK, 1) + kprev[...]
    off = lax.rem(36 * h, 16)
    pick = both
    for o in (4, 8, 12):
        pick = jnp.where(off == o, pltpu.roll(both, KROWS - o, 0), pick)
    kg_v[...] = pick[:36, :TOK]

    @pl.when(jnp.logical_not(final))
    def _():
        halo.wait_send()

    @pl.when(jnp.logical_not(first))
    def _():
        kp.wait_send()

    for d in range(1, NH):
        k_copy(d).wait_send()
    for g in range(4):
        for m in range(len(STEPS)):
            message(g, m).wait_send()
    for part_id in range(2):
        pos = y if part_id == 0 else x
        for d in range(1, L):
            p2(part_id, lax.rem(pos + d, L), pos).wait_send()


def hand_out(dq, kg, wg, dq_to, kg_to, wg_to, sem):
    copies = [
        pltpu.make_async_copy(src, dst, sem.at[i])
        for i, (src, dst) in enumerate(((dq, dq_to), (kg, kg_to), (wg, wg_to)))
    ]
    for cp in copies:
        cp.start()
    for cp in copies:
        cp.wait()


def shards(queries, latent_keys, out_grad, up_weight, segment_ids):
    vm, dma = pltpu.VMEM, pltpu.SemaphoreType.DMA
    dq, kg, wg = pl.pallas_call(
        kernel,
        out_shape=(
            jax.ShapeDtypeStruct((TOK * HD, NOPE + ROPE), F32),
            jax.ShapeDtypeStruct((36, TOK), F32),
            jax.ShapeDtypeStruct((64, KVD), F32),
        ),
        in_specs=[pl.BlockSpec(memory_space=pltpu.HBM)] * 5,
        out_specs=[pl.BlockSpec(memory_space=pltpu.VMEM)] * 3,
        scratch_shapes=[
            vm((TOK * HD, NOPE + ROPE), BF16),
            vm((TOK * HD, VDIM), BF16),
            vm((LAT * HD, KVD), BF16),
            vm((32, 128), jnp.int32),
            vm((WIN, LAT + ROPE), BF16),
            vm((2, LAT, 128), F32),
            vm((HD, LAT, KVD), BF16),
            vm((2, TOK * HD, 128), F32),
            vm((TOK * HD, VDIM), F32),
            vm((2, TOK * HD, 128), F32),
            vm((HD, WIN, KVD), BF16),
            vm((HD, WIN, KVD), BF16),
            vm((HD * TOK, WIN), BF16),
            vm((HD * TOK, 128), BF16),
            vm((LAT + ROPE, WIN), F32),
            vm((LAT + ROPE, WIN), BF16),
            vm((2, L, L, 16, 512), BF16),
            vm((4, 10, 2, 16, 512), BF16),
            vm((4, L, 16, 512), BF16),
            vm((2, L, 16, 512), BF16),
            vm((NH, KROWS, WIN), BF16),
            vm((KROWS, WIN), F32),
            vm((KROWS, WIN), F32),
            vm((2, 16, 512), F32),
            vm((2, 64, 128), F32),
            pltpu.SemaphoreType.REGULAR,
            pltpu.SemaphoreType.REGULAR,
            dma((5,)),
            dma((2,)),
            dma((4, len(STEPS))),
            dma((4, len(STEPS))),
            dma((2, L)),
            dma((2, L)),
            dma((NH,)),
            dma((NH,)),
            dma((2,)),
        ],
        compiler_params=pltpu.CompilerParams(
            collective_id=0, has_side_effects=True, vmem_limit_bytes=32 * 1024 * 1024
        ),
        name="mla_backward",
    )(
        *(
            pltpu.with_memory_space_constraint(a, pltpu.HBM)
            for a in (
                queries.reshape(TOK * HD, NOPE + ROPE),
                latent_keys,
                out_grad.reshape(TOK * HD, VDIM),
                up_weight.reshape(LAT * HD, KVD),
                segment_ids.reshape(32, 128),
            )
        )
    )
    dq, kg, wg = pl.pallas_call(
        hand_out,
        out_shape=tuple(jax.ShapeDtypeStruct(a.shape, a.dtype) for a in (dq, kg, wg)),
        in_specs=[pl.BlockSpec(memory_space=pl.ANY)] * 3,
        out_specs=[pl.BlockSpec(memory_space=pl.ANY)] * 3,
        scratch_shapes=[dma((3,))],
        compiler_params=pltpu.CompilerParams(vmem_limit_bytes=8 * 1024 * 1024),
        name="hand_out",
    )(dq, kg, wg)
    return (
        dq.reshape(TOK, HD, NOPE + ROPE),
        kg.T,
        wg.reshape(8, HD, KVD),
    )


def solution(mesh):
    return jax.shard_map(
        shards,
        mesh=mesh,
        in_specs=(
            P("ctx", "head", None),
            P("ctx", None),
            P("ctx", "head", None),
            P(None, "head", None),
            P(),
        ),
        out_specs=(P("ctx", "head", None), P("ctx", "head"), P("ctx", "head", None)),
        check_vma=False,
    )
```

```python
import math

import jax
import jax.numpy as jnp
from jax import lax
from jax.experimental import pallas as pl
from jax.experimental.pallas import tpu as pltpu
from jax.sharding import PartitionSpec as P

LAT = 512
ROPE = 64
NOPE = 128
VDIM = 128
KVD = NOPE + VDIM
TOK = 64
WIN = 128
HD = 8
L = 8
NH = 16
KROWS = 48
MESH = pl.DeviceIdType.MESH
F32 = jnp.float32
BF16 = jnp.bfloat16

STEPS = (
    (4, 0), (4, 1), (3, 2), (3, 3), (3, 0), (3, 1), (2, 2),
    (2, 3), (2, 0), (2, 1), (1, 2), (1, 3), (1, 0), (1, 1),
)
LAG = 4


def dot(a, b, ca, cb):
    return lax.dot_general(a, b, (((ca,), (cb,)), ((), ())), preferred_element_type=F32)


def kernel(
    q_hbm, lat_hbm, do_hbm, w_hbm, seg_hbm,
    dq_v, kg_v, wg_v,
    q_v, do_v, w_v, seg_v, latwin,
    wf, wflat, qf, dof, dqf,
    kv_v, dkv_v, ds_v, qr_v, kt32, kt16,
    term, ring, fin, part, kr, kpart, kprev, wgf, wgs,
    plane_sem, z_sem, in_sem, halo_sem, ring_send, ring_recv, p2_send, p2_recv, k_send, k_recv, kp_sem,
):
    c = lax.axis_index("ctx")
    h = lax.axis_index("head")
    y = lax.div(c, L)
    x = lax.rem(c, L)
    nxt = lax.rem(c + 1, L * L)
    prv = lax.rem(c + L * L - 1, L * L)

    def ctx_of(yy, xx):
        return yy * L + xx

    lat_cp = pltpu.make_async_copy(lat_hbm, latwin.at[pl.ds(TOK, TOK)], in_sem.at[0])
    w_cp = pltpu.make_async_copy(w_hbm, w_v, in_sem.at[1])
    q_cp = pltpu.make_async_copy(q_hbm, q_v, in_sem.at[2])
    do_cp = pltpu.make_async_copy(do_hbm, do_v, in_sem.at[3])
    seg_cp = pltpu.make_async_copy(seg_hbm, seg_v, in_sem.at[4])
    for cp in (lat_cp, q_cp, do_cp, seg_cp, w_cp):
        cp.start()

    odd_x = lax.rem(c, 2)
    even_ctx = c - odd_x
    odd_ctx = even_ctx + 1
    z = lax.div(h, 2)
    barrier = pltpu.get_barrier_semaphore()

    def greet(to):
        gate = to - lax.rem(to, 2)

        @pl.when(gate != c)
        def _():
            pl.semaphore_signal(barrier, inc=1, device_id=(gate, h), device_id_type=MESH)

    greet(nxt)
    greet(prv)
    for d in (1, L - 1):
        greet(ctx_of(y, lax.rem(x + d, L)))
        greet(ctx_of(lax.rem(y + d, L), x))
    for d in range(1, NH):
        pl.semaphore_signal(
            barrier, inc=1, device_id=(odd_ctx, lax.rem(h + d, NH)), device_id_type=MESH
        )

    lat_cp.wait()

    @pl.when(odd_x == 0)
    def _():
        pl.semaphore_wait(barrier, 10)
        pl.semaphore_signal(plane_sem, inc=1, device_id=(odd_ctx, h), device_id_type=MESH)

    @pl.when(odd_x == 1)
    def _():
        pl.semaphore_wait(plane_sem, 1)

    halo = pltpu.make_async_remote_copy(
        src_ref=latwin.at[pl.ds(TOK, TOK)],
        dst_ref=latwin.at[pl.ds(0, TOK)],
        send_sem=halo_sem.at[0],
        recv_sem=halo_sem.at[1],
        device_id=(nxt, h),
        device_id_type=MESH,
    )
    first, final = c == 0, c == L * L - 1

    @pl.when(jnp.logical_not(final))
    def _():
        halo.start()

    @pl.when(first)
    def _():
        latwin[:TOK, :] = jnp.zeros((TOK, LAT + ROPE), BF16)

    q_cp.wait()
    do_cp.wait()
    qf[1] = jnp.zeros((TOK * HD, 128), F32)
    qf[0] = q_v[:, :NOPE].astype(F32)
    qf[1, :, :ROPE] = q_v[:, NOPE:].astype(F32)
    dof[...] = do_v[...].astype(F32)
    qn, dob = [], []
    for hd in range(HD):
        qn.append(qf[0, pl.ds(hd, TOK, stride=HD), :].astype(BF16))
        qr_v[pl.ds(hd * TOK, TOK), :] = qf[1, pl.ds(hd, TOK, stride=HD), :].astype(BF16)
        dob.append(dof[pl.ds(hd, TOK, stride=HD), :].astype(BF16))

    w_cp.wait()
    rows = LAT * HD // 8

    def relayout(i, carry):
        base = pl.multiple_of(i * rows, rows)
        out = pl.multiple_of(i * (LAT // 8), LAT // 8)
        for half in range(2):
            wf[half] = w_v[pl.ds(base, rows), half * 128 : (half + 1) * 128].astype(F32)
        for hd in range(HD):
            for half in range(2):
                wflat[hd, pl.ds(out, LAT // 8), half * 128 : (half + 1) * 128] = wf[
                    half, pl.ds(hd, LAT // 8, stride=HD), :
                ].astype(BF16)
        return carry

    lax.fori_loop(0, 8, relayout, 0)

    seg_cp.wait()
    row = lax.div(c, 2)
    odd = lax.rem(c, 2)
    lane = lax.broadcasted_iota(jnp.int32, (1, WIN), 1)
    row_a = seg_v[pl.ds(row, 1), :]
    row_b = seg_v[pl.ds(jnp.maximum(row - 1, 0), 1), :]
    mixed = pltpu.roll(jnp.where(lane >= TOK, row_b, row_a), TOK, 1)
    seg_row = jnp.where(odd == 1, row_a, mixed)
    seg_row = jnp.where((lane < TOK) & (c == 0), -1, seg_row).astype(F32)
    seg_all = jnp.broadcast_to(seg_row, (WIN, WIN))
    seg_col = seg_all.T[TOK:, :]
    seg_all = seg_all[:TOK, :]
    pos_key = lax.broadcasted_iota(jnp.int32, (TOK, WIN), 1)
    pos_query = lax.broadcasted_iota(jnp.int32, (TOK, WIN), 0) + TOK
    visible = (seg_col == seg_all) & (pos_key <= pos_query)

    for hd in range(HD):
        kv_v[hd, TOK:, :] = dot(latwin[TOK:, :LAT], wflat[hd], 1, 0).astype(BF16)

    @pl.when(jnp.logical_not(first))
    def _():
        halo.wait_recv()

    for hd in range(HD):
        kv_v[hd, :TOK, :] = dot(latwin[:TOK, :LAT], wflat[hd], 1, 0).astype(BF16)

    k_rope = jnp.concatenate([latwin[:, LAT:], jnp.zeros((WIN, 128 - ROPE), BF16)], 1)
    scale = 1.0 / math.sqrt(NOPE + ROPE)
    scores, dprobs = [], []
    s_rope = dot(qr_v[...], k_rope, 1, 1)
    for hd in range(HD):
        key = kv_v[hd, :, :NOPE]
        val = kv_v[hd, :, NOPE:]
        scores.append(dot(qn[hd], key, 1, 1) + s_rope[hd * TOK : (hd + 1) * TOK])
        dprobs.append(dot(dob[hd], val, 1, 1))
    for hd in range(HD):
        s = jnp.where(visible, scores[hd] * scale, -1e30)
        top = jnp.max(s, -1, keepdims=True)
        expo = jnp.where(visible, jnp.exp(s - top), 0.0)
        probs = expo / jnp.sum(expo, -1, keepdims=True)
        delta = jnp.sum(probs * dprobs[hd], -1, keepdims=True)
        ds = (probs * (dprobs[hd] - delta) * scale).astype(BF16)
        p16 = probs.astype(BF16)
        ds_v[pl.ds(hd * TOK, TOK), :] = ds
        dkv_v[hd, :, :NOPE] = dot(ds, qn[hd], 0, 0).astype(BF16)
        dkv_v[hd, :, NOPE:] = dot(p16, dob[hd], 0, 0).astype(BF16)

    lat_t = latwin[:, :LAT].T

    def terms(part_id):
        for side in range(2):
            a = 4 * part_id + side
            lo = dot(lat_t, dkv_v[a], 1, 0).reshape(L * L, 8, KVD)
            hi = dot(lat_t, dkv_v[a + 2], 1, 0).reshape(L * L, 8, KVD)
            both = jnp.concatenate([lo, hi], 1).astype(BF16).reshape(L, L, 16, KVD)
            for i in range(L):
                block = both[:, i] if part_id == 0 else both[i]
                term[part_id, i, :, :, side * KVD : (side + 1) * KVD] = block

    def place(part_id, sign, dist):
        pos = x if part_id == 0 else y
        return lax.rem(pos + sign * dist + L, L)

    def neighbour(part_id, sign):
        if part_id == 0:
            return (ctx_of(y, lax.rem(x + sign + L, L)), h)
        return (ctx_of(lax.rem(y + sign + L, L), x), h)

    def message(g, m):
        part_id, back = g // 2, g % 2
        sign = -1 if back else 1
        dist, quarter = STEPS[m]
        quarter = quarter ^ (2 * back)
        src = term.at[part_id, place(part_id, sign, dist), pl.ds(2 * quarter, 2)]
        dst = fin.at[g, pl.ds(2 * quarter, 2)] if dist == 1 else ring.at[g, m]
        return pltpu.make_async_remote_copy(
            src_ref=src,
            dst_ref=dst,
            send_sem=ring_send.at[g, m],
            recv_sem=ring_recv.at[g, m],
            device_id=neighbour(part_id, sign),
            device_id_type=MESH,
        )

    def add(g, m):
        part_id, back = g // 2, g % 2
        sign = -1 if back else 1
        dist, quarter = STEPS[m]
        quarter = quarter ^ (2 * back)
        at = place(part_id, sign, dist)
        own = term[part_id, at, pl.ds(2 * quarter, 2)].astype(F32)
        term[part_id, at, pl.ds(2 * quarter, 2)] = (own + ring[g, m - LAG].astype(F32)).astype(
            BF16
        )

    def advance(lo, hi):
        for m in range(lo, hi):
            for g in range(4):
                message(g, m - LAG).wait_recv()
                add(g, m)
                message(g, m).start()

    for part_id in range(2):
        terms(part_id)
        for g in (2 * part_id, 2 * part_id + 1):
            for m in range(LAG):
                message(g, m).start()

    acc = dot(wflat[0], dkv_v[0], 1, 1)
    for hd in range(1, HD):
        acc = acc + dot(wflat[hd], dkv_v[hd], 1, 1)
    kt32[pl.ds(0, LAT), :] = acc
    kt32[pl.ds(LAT, ROPE), :] = dot(qr_v[...], ds_v[...], 0, 0)[:ROPE, :]
    kt16[...] = kt32[...].astype(BF16)

    def k_start(to):
        return pl.multiple_of(lax.div(36 * to, 16) * 16, 16)

    def k_copy(d):
        to = lax.rem(h + d, NH)
        return pltpu.make_async_remote_copy(
            src_ref=kt16.at[pl.ds(k_start(to), KROWS)],
            dst_ref=kr.at[d],
            send_sem=k_send.at[d],
            recv_sem=k_recv.at[d],
            device_id=(c, to),
            device_id_type=MESH,
        )

    def k_exchange():
        @pl.when(odd_x == 1)
        def _():
            pl.semaphore_wait(barrier, 2 * (NH - 1))
            pl.semaphore_signal(z_sem, inc=1, device_id=(even_ctx, h), device_id_type=MESH)

        @pl.when(odd_x == 0)
        def _():
            pl.semaphore_wait(z_sem, 1)

        for d in range(1, NH):
            k_copy(d).start()

    pl.when(z >= 4)(k_exchange)

    for hd in range(HD):
        ds = ds_v[pl.ds(hd * TOK, TOK), :]
        dqf[0, pl.ds(hd, TOK, stride=HD), :] = dot(ds, kv_v[hd, :, :NOPE], 1, 0)
        dqf[1, pl.ds(hd, TOK, stride=HD), :] = dot(ds, k_rope, 1, 0)
    dq_v[:, :NOPE] = dqf[0]
    dq_v[:, NOPE:] = dqf[1, :, :ROPE]

    advance(LAG, 10)
    pl.when(z < 4)(k_exchange)
    advance(10, len(STEPS))

    total = kt32[pl.ds(k_start(h), KROWS), :]
    for d in range(1, NH):
        k_copy(d).wait_recv()
        total = total + kr[d].astype(F32)
    kpart[...] = total
    kp = pltpu.make_async_remote_copy(
        src_ref=kpart,
        dst_ref=kprev,
        send_sem=kp_sem.at[0],
        recv_sem=kp_sem.at[1],
        device_id=(prv, h),
        device_id_type=MESH,
    )

    @pl.when(jnp.logical_not(first))
    def _():
        kp.start()

    def p2(part_id, to, frm):
        dev = (ctx_of(to, x), h) if part_id == 0 else (ctx_of(y, to), h)
        return pltpu.make_async_remote_copy(
            src_ref=term.at[part_id, x if part_id == 0 else y, to],
            dst_ref=part.at[part_id, frm],
            send_sem=p2_send.at[part_id, to],
            recv_sem=p2_recv.at[part_id, frm],
            device_id=dev,
            device_id_type=MESH,
        )

    def finish(part_id, quarter):
        mine = x if part_id == 0 else y
        pos = y if part_id == 0 else x
        at = pl.ds(2 * quarter, 2)
        summed = (
            term[part_id, mine, at].astype(F32)
            + fin[2 * part_id, at].astype(F32)
            + fin[2 * part_id + 1, at].astype(F32)
        )
        term[part_id, mine, at] = summed.astype(BF16)
        for j in range(2):
            to = 2 * quarter + j

            @pl.when(pos == to)
            def _():
                wgf[part_id] = summed[j]

            @pl.when(pos != to)
            def _():
                p2(part_id, to, pos).start()

    for last in range(2):
        for g in range(4):
            message(g, 10 + last).wait_recv()
            message(g, 12 + last).wait_recv()
        for part_id in range(2):
            finish(part_id, last)
            finish(part_id, 2 + last)

    for part_id in range(2):
        pos = y if part_id == 0 else x
        total = wgf[part_id]
        for d in range(1, L):
            frm = lax.rem(pos + d, L)
            p2(part_id, frm, frm).wait_recv()
            total = total + part[part_id, frm].astype(F32)
        for a in range(4):
            rows0 = (a // 2) * 8
            for half in range(2):
                cols = (a % 2) * KVD + half * 128
                wgs[half, pl.ds(4 * part_id + a, 8, stride=HD), :] = total[
                    rows0 : rows0 + 8, cols : cols + 128
                ]
    wg_v[:, :128] = wgs[0]
    wg_v[:, 128:] = wgs[1]

    @pl.when(jnp.logical_not(final))
    def _():
        kp.wait_recv()

    @pl.when(final)
    def _():
        kprev[...] = jnp.zeros((KROWS, WIN), F32)

    both = pltpu.roll(kpart[...], TOK, 1) + kprev[...]
    off = lax.rem(36 * h, 16)
    pick = both
    for o in (4, 8, 12):
        pick = jnp.where(off == o, pltpu.roll(both, KROWS - o, 0), pick)
    kg_v[...] = pick[:36, :TOK]

    @pl.when(jnp.logical_not(final))
    def _():
        halo.wait_send()

    @pl.when(jnp.logical_not(first))
    def _():
        kp.wait_send()

    for d in range(1, NH):
        k_copy(d).wait_send()
    for g in range(4):
        for m in range(len(STEPS)):
            message(g, m).wait_send()
    for part_id in range(2):
        pos = y if part_id == 0 else x
        for d in range(1, L):
            p2(part_id, lax.rem(pos + d, L), pos).wait_send()


def hand_out(dq, kg, wg, dq_to, kg_to, wg_to, sem):
    copies = [
        pltpu.make_async_copy(src, dst, sem.at[i])
        for i, (src, dst) in enumerate(((dq, dq_to), (kg, kg_to), (wg, wg_to)))
    ]
    for cp in copies:
        cp.start()
    for cp in copies:
        cp.wait()


def shards(queries, latent_keys, out_grad, up_weight, segment_ids):
    vm, dma = pltpu.VMEM, pltpu.SemaphoreType.DMA
    dq, kg, wg = pl.pallas_call(
        kernel,
        out_shape=(
            jax.ShapeDtypeStruct((TOK * HD, NOPE + ROPE), F32),
            jax.ShapeDtypeStruct((36, TOK), F32),
            jax.ShapeDtypeStruct((64, KVD), F32),
        ),
        in_specs=[pl.BlockSpec(memory_space=pltpu.HBM)] * 5,
        out_specs=[pl.BlockSpec(memory_space=pltpu.VMEM)] * 3,
        scratch_shapes=[
            vm((TOK * HD, NOPE + ROPE), BF16),
            vm((TOK * HD, VDIM), BF16),
            vm((LAT * HD, KVD), BF16),
            vm((32, 128), jnp.int32),
            vm((WIN, LAT + ROPE), BF16),
            vm((2, LAT, 128), F32),
            vm((HD, LAT, KVD), BF16),
            vm((2, TOK * HD, 128), F32),
            vm((TOK * HD, VDIM), F32),
            vm((2, TOK * HD, 128), F32),
            vm((HD, WIN, KVD), BF16),
            vm((HD, WIN, KVD), BF16),
            vm((HD * TOK, WIN), BF16),
            vm((HD * TOK, 128), BF16),
            vm((LAT + ROPE, WIN), F32),
            vm((LAT + ROPE, WIN), BF16),
            vm((2, L, L, 16, 512), BF16),
            vm((4, 10, 2, 16, 512), BF16),
            vm((4, L, 16, 512), BF16),
            vm((2, L, 16, 512), BF16),
            vm((NH, KROWS, WIN), BF16),
            vm((KROWS, WIN), F32),
            vm((KROWS, WIN), F32),
            vm((2, 16, 512), F32),
            vm((2, 64, 128), F32),
            pltpu.SemaphoreType.REGULAR,
            pltpu.SemaphoreType.REGULAR,
            dma((5,)),
            dma((2,)),
            dma((4, len(STEPS))),
            dma((4, len(STEPS))),
            dma((2, L)),
            dma((2, L)),
            dma((NH,)),
            dma((NH,)),
            dma((2,)),
        ],
        compiler_params=pltpu.CompilerParams(
            collective_id=0, has_side_effects=True, vmem_limit_bytes=32 * 1024 * 1024
        ),
        name="mla_backward",
    )(
        *(
            pltpu.with_memory_space_constraint(a, pltpu.HBM)
            for a in (
                queries.reshape(TOK * HD, NOPE + ROPE),
                latent_keys,
                out_grad.reshape(TOK * HD, VDIM),
                up_weight.reshape(LAT * HD, KVD),
                segment_ids.reshape(32, 128),
            )
        )
    )
    dq, kg, wg = pl.pallas_call(
        hand_out,
        out_shape=tuple(jax.ShapeDtypeStruct(a.shape, a.dtype) for a in (dq, kg, wg)),
        in_specs=[pl.BlockSpec(memory_space=pl.ANY)] * 3,
        out_specs=[pl.BlockSpec(memory_space=pl.ANY)] * 3,
        scratch_shapes=[dma((3,))],
        compiler_params=pltpu.CompilerParams(vmem_limit_bytes=8 * 1024 * 1024),
        name="hand_out",
    )(dq, kg, wg)
    return (
        dq.reshape(TOK, HD, NOPE + ROPE),
        kg.T,
        wg.reshape(8, HD, KVD),
    )


def solution(mesh):
    return jax.shard_map(
        shards,
        mesh=mesh,
        in_specs=(
            P("ctx", "head", None),
            P("ctx", None),
            P("ctx", "head", None),
            P(None, "head", None),
            P(),
        ),
        out_specs=(P("ctx", "head", None), P("ctx", "head"), P("ctx", "head", None)),
        check_vma=False,
    )
```
